768 devices in a mesh: cells: 192 (over y_lo, x, z), bands: 4 (over y_hi, core).
Axes of the slice: x: 4, y: 8 (y_hi: 2, y_lo: 4; y = y_hi * 4 + y_lo), z: 12, core: 2. Of those that a mesh axis runs over, the one named last changes fastest.
Arguments:
- wavefunctions: bfloat16 [139968, 512], P('cells', 'bands'), may hold values from -6 to 6
- hamiltonians: bfloat16 [192, 729, 729], P('cells'), may hold values from -0.21875 to 0.21875
- connectivity: int32 [192, 729], P('cells'), may hold values from 0 to 728, as said below
- face_nodes: int32 [384, 81], P('cells'), may hold values from 0 to 728, as said below
Outputs:
- filtered: float32 [139968, 512], P('cells', 'bands')
- correlation: float32 [512, 512], P(None, 'bands')
The draws below stay inside these ranges and needn't reach their ends.
Inputs may be any that keep to these rules, and one draw needn't show every extreme that they name: `connectivity`: within each partition the values are a permutation of the local node numbers laid on a lattice: cell c's node (i, j, k), 0 <= i, j, k <= 8, is lattice point (8 c + i, j, k) of the partition, so consecutive cells of a partition share 81 nodes and every local node belongs to some cell. `face_nodes`: row 0 of a partition lists the local numbers of its lattice points with first coordinate 0, row 1 those with first coordinate 8, in the order of the other two coordinates; neighbouring partitions list the same physical face nodes in the same order.
All inputs are finite; a program needn't handle non-finite values.
Results may differ from the reference program's by a relative error of at most 0.0039.
Values may be sent and summed in bfloat16 or wider, within the bound.
A program may use at most 32 MiB of HBM per device.

```python
import jax
import jax.numpy as jnp
from jax import lax

ORDER = 8
STEPS = 2
CELL_NODES = 729
SHARED = 81
CELLS_DEV = 1
NODES_DEV = 729
PARTITIONS = 192
BANDS = 512


def node_permutations(key):
    base_key = jax.random.fold_in(key, 11)
    part_keys = jax.vmap(lambda position: jax.random.fold_in(base_key, position))(jnp.arange(PARTITIONS, dtype=jnp.int32))
    return jax.vmap(lambda part_key: jax.random.permutation(part_key, NODES_DEV))(part_keys).astype(jnp.int32)


def draw_connectivity(key, part):
    node_perms = node_permutations(key)
    cell_ids = jnp.arange(CELLS_DEV, dtype=jnp.int32)[:, None]
    local_ids = jnp.arange(CELL_NODES, dtype=jnp.int32)[None, :]
    layer_x = local_ids // SHARED
    plane_pos = local_ids % SHARED
    lattice = (ORDER * cell_ids + layer_x) * SHARED + plane_pos
    return node_perms[:, lattice].reshape(PARTITIONS * CELLS_DEV, CELL_NODES).astype(jnp.int32)


def draw_face_nodes(key, part):
    node_perms = node_permutations(key)
    low_face = node_perms[:, :SHARED]
    high_face = node_perms[:, ORDER * CELLS_DEV * SHARED:]
    return jnp.stack([low_face, high_face], axis=1).reshape(PARTITIONS * 2, SHARED).astype(jnp.int32)


def shard_levels(own_key, shape, pieces, least, high):
    level = 1.0
    for axis_at, blocks in pieces:
        draws = jax.random.uniform(jax.random.fold_in(jax.random.fold_in(own_key, 6), axis_at), (blocks,), jnp.float32, least / len(pieces), high / len(pieces))
        level = level * jnp.repeat(jnp.exp(draws), shape[axis_at] // blocks).reshape((-1,) + (1,) * (len(shape) - 1 - axis_at))
    return level


def gaussian(key, extent, width, bound, pieces=(), held_as=jnp.bfloat16):
    loudness = shard_levels(key, extent, pieces, -0.22, 0.18) if pieces else 1.0
    values = jax.random.normal(key, extent, jnp.float32) * width * loudness
    return jnp.minimum(jnp.maximum(values, -bound), bound).astype(held_as)


def setup_inputs(seed: int = 0) -> dict:
    key_list = jax.random.split(jax.random.key(seed), 5)
    return {
        "wavefunctions": gaussian(key_list[0], (PARTITIONS * NODES_DEV, BANDS), 1.0, 6.0, ((0, 192), (1, 4))),
        "hamiltonians": gaussian(key_list[1], (PARTITIONS * CELLS_DEV, CELL_NODES, CELL_NODES), CELL_NODES ** -0.5, 0.21875, ((0, 192),)),
        "connectivity": draw_connectivity(jax.random.fold_in(key_list[4], 71), 0),
        "face_nodes": draw_face_nodes(jax.random.fold_in(key_list[4], 71), 0),
    }


def apply_local(vector_bf, cell_hams, cell_nodes):
    def one_part(entries):
        values, hams_part, nodes_part = entries
        gathered = values[nodes_part].astype(jnp.float32)
        cell_terms = jnp.einsum('cij,cjb->cib', hams_part.astype(jnp.float32), gathered, precision=lax.Precision.HIGHEST)
        summed = jnp.zeros((NODES_DEV, BANDS), jnp.float32)
        return summed.at[nodes_part.reshape(-1)].add(cell_terms.reshape(-1, BANDS))
    return lax.map(one_part, (vector_bf, cell_hams, cell_nodes))


def assemble(local_sums, face_index):
    face_vals = jax.vmap(lambda values, rows: values[rows])(local_sums, face_index)
    zero_face = jnp.zeros((1, SHARED, BANDS), jnp.float32)
    from_before = jnp.concatenate([zero_face, face_vals[:-1, 1]], axis=0)
    from_after = jnp.concatenate([face_vals[1:, 0], zero_face], axis=0)

    def add_faces(values, rows, before, after):
        return values.at[rows[0]].add(before).at[rows[1]].add(after)
    return jax.vmap(add_faces)(local_sums, face_index, from_before, from_after)


def reference(wavefunctions, hamiltonians, connectivity, face_nodes):
    start_vec = wavefunctions.reshape(PARTITIONS, NODES_DEV, BANDS).astype(jnp.float32)
    cell_hams = hamiltonians.reshape(PARTITIONS, CELLS_DEV, CELL_NODES, CELL_NODES)
    cell_nodes = connectivity.reshape(PARTITIONS, CELLS_DEV, CELL_NODES)
    face_index = face_nodes.reshape(PARTITIONS, 2, SHARED)

    def operate(vector):
        return assemble(apply_local(vector.astype(jnp.bfloat16), cell_hams, cell_nodes), face_index)

    older = start_vec
    newer = 0.5 * operate(start_vec)
    for step in range(STEPS - 1):
        following = operate(newer) - older
        older = newer
        newer = following
    filtered = newer.reshape(PARTITIONS * NODES_DEV, BANDS)

    def keep_part(position, rows):
        value = jnp.where(position > 0, jnp.float32(0.0), jnp.float32(1.0))
        return jnp.ones((NODES_DEV,), jnp.float32).at[rows].set(value)
    keep_rows = jax.vmap(keep_part)(jnp.arange(PARTITIONS, dtype=jnp.int32), face_index[:, 0])
    masked = newer * keep_rows[:, :, None]

    def add_part(gram_sum, values):
        high_word = values.astype(jnp.bfloat16)
        term = jnp.dot(high_word.T, high_word, preferred_element_type=jnp.float32)
        return gram_sum + term, None

    gram, unused = lax.scan(add_part, jnp.zeros((BANDS, BANDS), jnp.float32), masked)
    correlation = gram / (PARTITIONS * NODES_DEV)
    return filtered, correlation
```

```python
import jax
import jax.numpy as jnp
from jax import lax
from jax.experimental import pallas as pl
from jax.experimental.pallas import tpu as pltpu
from jax.sharding import PartitionSpec as P

MESH = pl.DeviceIdType.MESH
NODES = 729
SHARED = 81
FAR = NODES - SHARED
WIDTH = 128
EARLY = 640
ROWS = 736
F32 = jnp.float32
BF16 = jnp.bfloat16


def mm(a, b):
    return jnp.dot(a, b, preferred_element_type=F32)


def kernel(
    sizes,
    v_hbm, h_hbm, conn_hbm,
    out_hbm, corr_ref,
    v, h, conn, u, t, y1, filt, fall, face_out, face_in,
    gram_f, gram_b, rx, ry_out, ry, rz, res,
    in_sem, out_sem, face_send, face_recv, f_send, f_recv, w_send, w_recv,
    x_send, x_recv, y_send, y_recv, z_send, z_recv, ay_send, ay_recv, ax_send, ax_recv,
):
    ny, nx, nz = sizes
    cells = lax.axis_index("cells")
    band = lax.axis_index("bands")
    last = ny * nx * nz - 1
    z = lax.rem(cells, nz)
    x = lax.rem(cells // nz, nx)
    y = cells // (nx * nz)
    core = lax.rem(band, 2)
    ring = 2 * ny
    half = ny // 2
    here = (band // 2) * ny + y

    def at(yy, xx, zz):
        return (yy * nx + xx) * nz + zz

    def f_peer(offset):
        there = lax.rem(here + offset + ring, ring)
        return (at(lax.rem(there, ny), x, z), (there // ny) * 2 + core)

    f_peers = [f_peer(half), f_peer(-half)]
    twin = (cells, band + 1 - 2 * core)
    x_peers = [(at(y, lax.rem(x + k, nx), z), band) for k in range(1, nx)]
    y_peers = [(at(lax.rem(y + k, ny), x, z), band) for k in range(1, ny)]
    z_peers = [(at(y, x, lax.rem(z + k, nz)), band) for k in range(1, nz)]

    loads = [
        pltpu.make_async_copy(conn_hbm, conn, in_sem.at[0]),
        pltpu.make_async_copy(v_hbm, v, in_sem.at[1]),
        pltpu.make_async_copy(h_hbm.at[0], h, in_sem.at[2]),
    ]
    for load in loads:
        load.start()

    barrier = pltpu.get_barrier_semaphore()
    peers = f_peers + [twin] + x_peers + y_peers + z_peers
    for peer in peers:
        pl.semaphore_signal(barrier, inc=1, device_id=peer, device_id_type=MESH)

    @pl.when(cells > 0)
    def _():
        pl.semaphore_signal(barrier, inc=1, device_id=(cells - 1, band), device_id_type=MESH)

    @pl.when(cells < last)
    def _():
        pl.semaphore_signal(barrier, inc=1, device_id=(cells + 1, band), device_id_type=MESH)

    def face_copy(step, side):
        peer = (cells - 1 + 2 * side, band)
        return pltpu.make_async_remote_copy(
            face_out.at[step, side], face_in.at[step, 1 - side],
            face_send.at[step, side], face_recv.at[step, 1 - side],
            device_id=peer, device_id_type=MESH,
        )

    def send_faces(step):
        @pl.when(cells > 0)
        def _():
            face_copy(step, 0).start()

        @pl.when(cells < last)
        def _():
            face_copy(step, 1).start()

    def wait_faces(step):
        @pl.when(cells > 0)
        def _():
            face_copy(step, 1).wait_recv()

        @pl.when(cells < last)
        def _():
            face_copy(step, 0).wait_recv()

    def done_faces(step):
        @pl.when(cells > 0)
        def _():
            face_copy(step, 0).wait_send()

        @pl.when(cells < last)
        def _():
            face_copy(step, 1).wait_send()

    @pl.when(cells == 0)
    def _():
        for step in range(2):
            face_in[step, 0] = jnp.zeros(face_in.shape[2:], BF16)

    @pl.when(cells == last)
    def _():
        for step in range(2):
            face_in[step, 1] = jnp.zeros(face_in.shape[2:], BF16)

    loads[0].wait()
    order = conn[...].astype(F32)
    column = jnp.broadcast_to(order, (WIDTH, NODES)).T
    lanes = lax.broadcasted_iota(jnp.int32, (NODES, WIDTH), 1).astype(F32)
    loads[1].wait()
    total = jnp.zeros((NODES, WIDTH), F32)
    for k in range(0, NODES, WIDTH):
        width = min(WIDTH, NODES - k)
        pick = jnp.where(column == lanes + float(k), 1.0, 0.0).astype(BF16)
        total += mm(pick[:, :width], v[k:k + width, :])
    u[0:NODES, :] = total.astype(BF16)

    loads[2].wait()
    t[0:96, :] = mm(h[0:96, :], u[0:NODES, :])
    t[EARLY:NODES, :] = mm(h[EARLY:NODES, :], u[0:NODES, :])
    face_out[0, 0, 0:SHARED, :] = t[0:SHARED, :].astype(BF16)
    face_out[0, 1, 0:SHARED, :] = t[FAR:NODES, :].astype(BF16)
    want = len(peers) + jnp.where(cells > 0, 1, 0) + jnp.where(cells < last, 1, 0)
    pl.semaphore_wait(barrier, want)
    send_faces(0)
    t[96:EARLY, :] = mm(h[96:EARLY, :], u[0:NODES, :])
    y1[0:NODES, :] = (0.5 * t[0:NODES, :]).astype(BF16)
    y1[0:SHARED, :] = jnp.zeros((SHARED, WIDTH), BF16)
    y1[FAR:NODES, :] = jnp.zeros((SHARED, WIDTH), BF16)
    low = t[0:SHARED, :]
    high = t[FAR:NODES, :]
    t[0:NODES, :] = mm(h[...], y1[0:NODES, :])

    wait_faces(0)
    low1 = 0.5 * (low + face_in[0, 0, 0:SHARED, :].astype(F32))
    high1 = 0.5 * (high + face_in[0, 1, 0:SHARED, :].astype(F32))
    y1[0:WIDTH, :] = jnp.zeros((WIDTH, WIDTH), BF16)
    y1[EARLY:NODES, :] = jnp.zeros((NODES - EARLY, WIDTH), BF16)
    y1[0:SHARED, :] = low1.astype(BF16)
    y1[FAR:NODES, :] = high1.astype(BF16)

    def add_faces(lo, hi):
        t[lo:hi, :] += mm(h[lo:hi, 0:WIDTH], y1[0:WIDTH, :]) + mm(h[lo:hi, EARLY:NODES], y1[EARLY:NODES, :])

    add_faces(0, 96)
    add_faces(EARLY, NODES)
    face_out[1, 0, 0:SHARED, :] = t[0:SHARED, :].astype(BF16)
    face_out[1, 1, 0:SHARED, :] = t[FAR:NODES, :].astype(BF16)
    send_faces(1)
    add_faces(96, EARLY)

    first = jnp.where(cells == 0, jnp.float32(1.0), jnp.float32(0.0))
    t[0:NODES, :] = t[0:NODES, :] - u[0:NODES, :].astype(F32)
    filt[0:NODES, :] = t[0:NODES, :].astype(BF16)
    filt[0:SHARED, :] = (t[0:SHARED, :] * first).astype(BF16)

    def f_copy(part, k):
        rows = pl.ds(0, EARLY) if part == 0 else pl.ds(EARLY, ROWS - EARLY)
        return pltpu.make_async_remote_copy(
            filt.at[rows], fall.at[band, rows],
            f_send.at[part, k], f_recv.at[part, k],
            device_id=f_peers[k], device_id_type=MESH,
        )

    for k in range(2):
        f_copy(0, k).start()

    wait_faces(1)
    t[0:SHARED, :] += face_in[1, 0, 0:SHARED, :].astype(F32)
    t[FAR:NODES, :] += face_in[1, 1, 0:SHARED, :].astype(F32)
    filt[EARLY:NODES, :] = t[EARLY:NODES, :].astype(BF16)
    filt[NODES:ROWS, :] = jnp.zeros((ROWS - NODES, WIDTH), BF16)
    for k in range(2):
        f_copy(1, k).start()

    rows = lax.broadcasted_iota(jnp.int32, (NODES, NODES), 0).astype(F32)
    place = jnp.where(rows == jnp.broadcast_to(order, (NODES, NODES)), 1.0, 0.0).astype(BF16)
    full = t[0:NODES, :]
    coarse = full.astype(BF16)
    fine = (full - coarse.astype(F32)).astype(BF16)
    t[0:NODES, :] = mm(place, coarse) + mm(place, fine)
    store = pltpu.make_async_copy(t.at[pl.ds(0, NODES)], out_hbm, out_sem)
    store.start()

    def w_copy(part, k):
        rows = pl.ds(0, EARLY) if part == 0 else pl.ds(EARLY, ROWS - EARLY)
        slot = (lax.rem(here - half * (1 - 2 * k) + ring, ring) // ny) * 2 + core
        return pltpu.make_async_remote_copy(
            fall.at[slot, rows], fall.at[slot, rows],
            w_send.at[part, k], w_recv.at[part, k],
            device_id=twin, device_id_type=MESH,
        )

    for part in range(2):
        for k in range(2):
            f_copy(part, k).wait_recv()
            w_copy(part, k).start()
    for part in range(2):
        for k in range(2):
            w_copy(part, k).wait_recv()

    mine = fall[band]
    for j in range(4):
        block = lax.dot_general(mine, fall[j], (((0,), (0,)), ((), ())), preferred_element_type=F32)
        gram_f[j] = block
        gram_b[j] = block.astype(BF16)

    x_copies = []
    for k in range(1, nx):
        copy = pltpu.make_async_remote_copy(
            gram_b.at[lax.rem(x + k, nx)], rx.at[k - 1],
            x_send.at[k - 1], x_recv.at[k - 1],
            device_id=x_peers[k - 1], device_id_type=MESH,
        )
        copy.start()
        x_copies.append(copy)
    part_sum = gram_f[x]
    for k in range(1, nx):
        x_copies[k - 1].wait_recv()
        part_sum += rx[k - 1].astype(F32)

    piece = WIDTH // ny
    gram_f[0] = part_sum
    ry_out[...] = part_sum.astype(BF16)
    y_copies = []
    for k in range(1, ny):
        copy = pltpu.make_async_remote_copy(
            ry_out.at[pl.ds(pl.multiple_of(lax.rem(y + k, ny) * piece, piece), piece)], ry.at[k - 1],
            y_send.at[k - 1], y_recv.at[k - 1],
            device_id=y_peers[k - 1], device_id_type=MESH,
        )
        copy.start()
        y_copies.append(copy)
    my_rows = pl.ds(pl.multiple_of(y * piece, piece), piece)
    shard = gram_f[0, my_rows, :]
    for k in range(1, ny):
        y_copies[k - 1].wait_recv()
        shard += ry[k - 1].astype(F32)

    rz[z] = shard.astype(BF16)
    z_copies = []
    for k in range(1, nz):
        copy = pltpu.make_async_remote_copy(
            rz.at[z], rz.at[z],
            z_send.at[k - 1], z_recv.at[k - 1],
            device_id=z_peers[k - 1], device_id_type=MESH,
        )
        copy.start()
        z_copies.append(copy)
    for copy in z_copies:
        copy.wait_recv()
    summed = rz[0].astype(F32)
    for k in range(1, nz):
        summed += rz[k].astype(F32)
    res[x, my_rows, :] = (summed / float((last + 1) * NODES)).astype(BF16)

    ay_copies = []
    for k in range(1, ny):
        copy = pltpu.make_async_remote_copy(
            res.at[x, my_rows], res.at[x, my_rows],
            ay_send.at[k - 1], ay_recv.at[k - 1],
            device_id=y_peers[k - 1], device_id_type=MESH,
        )
        copy.start()
        ay_copies.append(copy)
    for copy in ay_copies:
        copy.wait_recv()
    ax_copies = []
    for k in range(1, nx):
        copy = pltpu.make_async_remote_copy(
            res.at[x], res.at[x],
            ax_send.at[k - 1], ax_recv.at[k - 1],
            device_id=x_peers[k - 1], device_id_type=MESH,
        )
        copy.start()
        ax_copies.append(copy)
    for copy in ax_copies:
        copy.wait_recv()
    for j in range(4):
        corr_ref[j * WIDTH:(j + 1) * WIDTH, :] = res[j].astype(F32).T

    done_faces(0)
    done_faces(1)
    for part in range(2):
        for k in range(2):
            f_copy(part, k).wait_send()
            w_copy(part, k).wait_send()
    for copy in x_copies + y_copies + z_copies + ay_copies + ax_copies:
        copy.wait_send()
    store.wait()


def solution(mesh, sizes=(4, 4, 12)):
    ny, nx, nz = sizes
    dma = pltpu.SemaphoreType.DMA

    def body(wavefunctions, hamiltonians, connectivity, face_nodes):
        return pl.pallas_call(
            lambda *refs: kernel(sizes, *refs),
            out_shape=(
                jax.ShapeDtypeStruct((NODES, WIDTH), F32),
                jax.ShapeDtypeStruct((4 * WIDTH, WIDTH), F32),
            ),
            in_specs=[pl.BlockSpec(memory_space=pl.ANY)] * 3,
            out_specs=(
                pl.BlockSpec(memory_space=pl.ANY),
                pl.BlockSpec(memory_space=pltpu.VMEM),
            ),
            scratch_shapes=[
                pltpu.VMEM((NODES, WIDTH), BF16),
                pltpu.VMEM((NODES, NODES), BF16),
                pltpu.VMEM((1, NODES), jnp.int32),
                pltpu.VMEM((ROWS, WIDTH), BF16),
                pltpu.VMEM((ROWS, WIDTH), F32),
                pltpu.VMEM((ROWS, WIDTH), BF16),
                pltpu.VMEM((ROWS, WIDTH), BF16),
                pltpu.VMEM((4, ROWS, WIDTH), BF16),
                pltpu.VMEM((2, 2, 96, WIDTH), BF16),
                pltpu.VMEM((2, 2, 96, WIDTH), BF16),
                pltpu.VMEM((4, WIDTH, WIDTH), F32),
                pltpu.VMEM((4, WIDTH, WIDTH), BF16),
                pltpu.VMEM((nx - 1, WIDTH, WIDTH), BF16),
                pltpu.VMEM((WIDTH, WIDTH), BF16),
                pltpu.VMEM((ny - 1, WIDTH // ny, WIDTH), BF16),
                pltpu.VMEM((nz, WIDTH // ny, WIDTH), BF16),
                pltpu.VMEM((4, WIDTH, WIDTH), BF16),
                dma((3,)), dma,
                dma((2, 2)), dma((2, 2)),
                dma((2, 2)), dma((2, 2)), dma((2, 2)), dma((2, 2)),
                dma((nx - 1,)), dma((nx - 1,)),
                dma((ny - 1,)), dma((ny - 1,)),
                dma((nz - 1,)), dma((nz - 1,)),
                dma((ny - 1,)), dma((ny - 1,)),
                dma((nx - 1,)), dma((nx - 1,)),
            ],
            compiler_params=pltpu.CompilerParams(
                collective_id=0, has_side_effects=True, vmem_limit_bytes=40 << 20
            ),
        )(wavefunctions, hamiltonians, connectivity)

    return jax.shard_map(
        body,
        mesh=mesh,
        in_specs=(P("cells", "bands"), P("cells", None, None), P("cells", None), P("cells", None)),
        out_specs=(P("cells", "bands"), P(None, "bands")),
        check_vma=False,
    )
```

```python
import jax
import jax.numpy as jnp
from jax import lax
from jax.experimental import pallas as pl
from jax.experimental.pallas import tpu as pltpu
from jax.sharding import PartitionSpec as P

MESH = pl.DeviceIdType.MESH
NODES = 729
SHARED = 81
FAR = NODES - SHARED
WIDTH = 128
EARLY = 640
ROWS = 736
F32 = jnp.float32
BF16 = jnp.bfloat16


def mm(a, b):
    return jnp.dot(a, b, preferred_element_type=F32)


def kernel(
    sizes,
    v_hbm, h_hbm, conn_hbm,
    out_ref, res,
    v, h, conn, u, t, y1, filt, fall, face_out, face_in,
    gram_f, gram_b, rx, ry_out, ry, rz,
    in_sem, face_send, face_recv, near, f_send, f_recv, w_send, w_recv,
    x_send, x_recv, y_send, y_recv, z_send, z_recv, ay_send, ay_recv, ax_send, ax_recv,
):
    ny, nx, nz = sizes
    cells = lax.axis_index("cells")
    band = lax.axis_index("bands")
    last = ny * nx * nz - 1
    z = lax.rem(cells, nz)
    x = lax.rem(cells // nz, nx)
    y = cells // (nx * nz)
    core = lax.rem(band, 2)
    ring = 2 * ny
    half = ny // 2
    here = (band // 2) * ny + y

    def at(yy, xx, zz):
        return (yy * nx + xx) * nz + zz

    def f_peer(offset):
        there = lax.rem(here + offset + ring, ring)
        return (at(lax.rem(there, ny), x, z), (there // ny) * 2 + core)

    f_peers = [f_peer(half), f_peer(-half)]
    twin = (cells, band + 1 - 2 * core)
    x_peers = [(at(y, lax.rem(x + k, nx), z), band) for k in range(1, nx)]
    y_peers = [(at(lax.rem(y + k, ny), x, z), band) for k in range(1, ny)]
    z_peers = [(at(y, x, lax.rem(z + k, nz)), band) for k in range(1, nz)]

    loads = [
        pltpu.make_async_copy(conn_hbm, conn, in_sem.at[0]),
        pltpu.make_async_copy(v_hbm, v, in_sem.at[1]),
        pltpu.make_async_copy(h_hbm.at[0], h, in_sem.at[2]),
    ]
    for load in loads:
        load.start()

    barrier = pltpu.get_barrier_semaphore()

    def z_peer(offset):
        return (at(y, x, lax.rem(z + offset + nz, nz)), band)

    peers = f_peers + [twin] + x_peers + y_peers + [z_peer(1), z_peer(-1)]

    def meet(stage):
        reach = (1, 2, 2)[stage]
        for side in range(2):
            pl.semaphore_signal(
                near.at[stage, side], inc=1, device_id=z_peer(reach * (1 - 2 * side)), device_id_type=MESH
            )

    def met(stage):
        for side in range(2):
            pl.semaphore_wait(near.at[stage, side], 1)

    for peer in peers:
        pl.semaphore_signal(barrier, inc=1, device_id=peer, device_id_type=MESH)

    @pl.when(cells > 0)
    def _():
        pl.semaphore_signal(barrier, inc=1, device_id=(cells - 1, band), device_id_type=MESH)

    @pl.when(cells < last)
    def _():
        pl.semaphore_signal(barrier, inc=1, device_id=(cells + 1, band), device_id_type=MESH)

    def face_copy(step, side):
        peer = (cells - 1 + 2 * side, band)
        return pltpu.make_async_remote_copy(
            face_out.at[step, side], face_in.at[step, 1 - side],
            face_send.at[step, side], face_recv.at[step, 1 - side],
            device_id=peer, device_id_type=MESH,
        )

    def send_faces(step):
        @pl.when(cells > 0)
        def _():
            face_copy(step, 0).start()

        @pl.when(cells < last)
        def _():
            face_copy(step, 1).start()

    def wait_faces(step):
        @pl.when(cells > 0)
        def _():
            face_copy(step, 1).wait_recv()

        @pl.when(cells < last)
        def _():
            face_copy(step, 0).wait_recv()

    def done_faces(step):
        @pl.when(cells > 0)
        def _():
            face_copy(step, 0).wait_send()

        @pl.when(cells < last)
        def _():
            face_copy(step, 1).wait_send()

    @pl.when(cells == 0)
    def _():
        for step in range(2):
            face_in[step, 0] = jnp.zeros(face_in.shape[2:], BF16)

    @pl.when(cells == last)
    def _():
        for step in range(2):
            face_in[step, 1] = jnp.zeros(face_in.shape[2:], BF16)

    loads[0].wait()
    order = conn[...].astype(F32)
    column = jnp.broadcast_to(order, (WIDTH, NODES)).T
    lanes = lax.broadcasted_iota(jnp.int32, (NODES, WIDTH), 1).astype(F32)
    loads[1].wait()
    total = jnp.zeros((NODES, WIDTH), F32)
    for k in range(0, NODES, WIDTH):
        width = min(WIDTH, NODES - k)
        pick = jnp.where(column == lanes + float(k), 1.0, 0.0).astype(BF16)
        total += mm(pick[:, :width], v[k:k + width, :])
    u[0:NODES, :] = total.astype(BF16)

    loads[2].wait()
    t[0:96, :] = mm(h[0:96, :], u[0:NODES, :])
    t[EARLY:NODES, :] = mm(h[EARLY:NODES, :], u[0:NODES, :])
    face_out[0, 0, 0:SHARED, :] = t[0:SHARED, :].astype(BF16)
    face_out[0, 1, 0:SHARED, :] = t[FAR:NODES, :].astype(BF16)
    want = len(peers) + jnp.where(cells > 0, 1, 0) + jnp.where(cells < last, 1, 0)
    pl.semaphore_wait(barrier, want)
    meet(0)
    send_faces(0)
    t[96:EARLY, :] = mm(h[96:EARLY, :], u[0:NODES, :])
    y1[0:NODES, :] = (0.5 * t[0:NODES, :]).astype(BF16)
    y1[0:SHARED, :] = jnp.zeros((SHARED, WIDTH), BF16)
    y1[FAR:NODES, :] = jnp.zeros((SHARED, WIDTH), BF16)
    low = t[0:SHARED, :]
    high = t[FAR:NODES, :]
    t[0:NODES, :] = mm(h[...], y1[0:NODES, :])

    wait_faces(0)
    met(0)
    meet(1)
    low1 = 0.5 * (low + face_in[0, 0, 0:SHARED, :].astype(F32))
    high1 = 0.5 * (high + face_in[0, 1, 0:SHARED, :].astype(F32))
    y1[0:WIDTH, :] = jnp.zeros((WIDTH, WIDTH), BF16)
    y1[EARLY:NODES, :] = jnp.zeros((NODES - EARLY, WIDTH), BF16)
    y1[0:SHARED, :] = low1.astype(BF16)
    y1[FAR:NODES, :] = high1.astype(BF16)

    def add_faces(lo, hi):
        t[lo:hi, :] += mm(h[lo:hi, 0:WIDTH], y1[0:WIDTH, :]) + mm(h[lo:hi, EARLY:NODES], y1[EARLY:NODES, :])

    add_faces(0, 96)
    add_faces(EARLY, NODES)
    face_out[1, 0, 0:SHARED, :] = t[0:SHARED, :].astype(BF16)
    face_out[1, 1, 0:SHARED, :] = t[FAR:NODES, :].astype(BF16)
    send_faces(1)
    add_faces(96, EARLY)

    first = jnp.where(cells == 0, jnp.float32(1.0), jnp.float32(0.0))
    t[0:NODES, :] = t[0:NODES, :] - u[0:NODES, :].astype(F32)
    filt[0:NODES, :] = t[0:NODES, :].astype(BF16)
    filt[0:SHARED, :] = (t[0:SHARED, :] * first).astype(BF16)

    def f_copy(part, k):
        rows = pl.ds(0, EARLY) if part == 0 else pl.ds(EARLY, ROWS - EARLY)
        return pltpu.make_async_remote_copy(
            filt.at[rows], fall.at[band, rows],
            f_send.at[part, k], f_recv.at[part, k],
            device_id=f_peers[k], device_id_type=MESH,
        )

    for k in range(2):
        f_copy(0, k).start()

    wait_faces(1)
    t[0:SHARED, :] += face_in[1, 0, 0:SHARED, :].astype(F32)
    t[FAR:NODES, :] += face_in[1, 1, 0:SHARED, :].astype(F32)
    filt[EARLY:NODES, :] = t[EARLY:NODES, :].astype(BF16)
    filt[NODES:ROWS, :] = jnp.zeros((ROWS - NODES, WIDTH), BF16)
    for k in range(2):
        f_copy(1, k).start()

    met(1)
    meet(2)

    rows = lax.broadcasted_iota(jnp.int32, (NODES, NODES), 0).astype(F32)
    place = jnp.where(rows == jnp.broadcast_to(order, (NODES, NODES)), 1.0, 0.0).astype(BF16)
    full = t[0:NODES, :]
    coarse = full.astype(BF16)
    fine = (full - coarse.astype(F32)).astype(BF16)
    out_ref[...] = mm(place, coarse) + mm(place, fine)

    def w_copy(part, k):
        rows = pl.ds(0, EARLY) if part == 0 else pl.ds(EARLY, ROWS - EARLY)
        slot = (lax.rem(here - half * (1 - 2 * k) + ring, ring) // ny) * 2 + core
        return pltpu.make_async_remote_copy(
            fall.at[slot, rows], fall.at[slot, rows],
            w_send.at[part, k], w_recv.at[part, k],
            device_id=twin, device_id_type=MESH,
        )

    for part in range(2):
        for k in range(2):
            f_copy(part, k).wait_recv()
            w_copy(part, k).start()
    for part in range(2):
        for k in range(2):
            w_copy(part, k).wait_recv()

    mine = fall[band]
    for j in range(4):
        block = lax.dot_general(mine, fall[j], (((0,), (0,)), ((), ())), preferred_element_type=F32)
        gram_f[j] = block
        gram_b[j] = block.astype(BF16)

    x_copies = []
    for k in range(1, nx):
        copy = pltpu.make_async_remote_copy(
            gram_b.at[lax.rem(x + k, nx)], rx.at[k - 1],
            x_send.at[k - 1], x_recv.at[k - 1],
            device_id=x_peers[k - 1], device_id_type=MESH,
        )
        copy.start()
        x_copies.append(copy)
    part_sum = gram_f[x]
    for k in range(1, nx):
        x_copies[k - 1].wait_recv()
        part_sum += rx[k - 1].astype(F32)

    piece = WIDTH // ny
    gram_f[0] = part_sum
    ry_out[...] = part_sum.astype(BF16)
    y_copies = []
    for k in range(1, ny):
        copy = pltpu.make_async_remote_copy(
            ry_out.at[pl.ds(pl.multiple_of(lax.rem(y + k, ny) * piece, piece), piece)], ry.at[k - 1],
            y_send.at[k - 1], y_recv.at[k - 1],
            device_id=y_peers[k - 1], device_id_type=MESH,
        )
        copy.start()
        y_copies.append(copy)
    my_rows = pl.ds(pl.multiple_of(y * piece, piece), piece)
    shard = gram_f[0, my_rows, :]
    for k in range(1, ny):
        y_copies[k - 1].wait_recv()
        shard += ry[k - 1].astype(F32)

    met(2)
    rz[z] = shard.astype(BF16)
    z_copies = []
    for k in range(1, nz):
        copy = pltpu.make_async_remote_copy(
            rz.at[z], rz.at[z],
            z_send.at[k - 1], z_recv.at[k - 1],
            device_id=z_peers[k - 1], device_id_type=MESH,
        )
        copy.start()
        z_copies.append(copy)
    for copy in z_copies:
        copy.wait_recv()
    summed = rz[0].astype(F32)
    for k in range(1, nz):
        summed += rz[k].astype(F32)
    res[x, my_rows, :] = (summed / float((last + 1) * NODES)).astype(BF16)

    ay_copies = []
    for k in range(1, ny):
        copy = pltpu.make_async_remote_copy(
            res.at[x, my_rows], res.at[x, my_rows],
            ay_send.at[k - 1], ay_recv.at[k - 1],
            device_id=y_peers[k - 1], device_id_type=MESH,
        )
        copy.start()
        ay_copies.append(copy)
    for copy in ay_copies:
        copy.wait_recv()
    ax_copies = []
    for k in range(1, nx):
        copy = pltpu.make_async_remote_copy(
            res.at[x], res.at[x],
            ax_send.at[k - 1], ax_recv.at[k - 1],
            device_id=x_peers[k - 1], device_id_type=MESH,
        )
        copy.start()
        ax_copies.append(copy)
    for copy in ax_copies:
        copy.wait_recv()
    done_faces(0)
    done_faces(1)
    for part in range(2):
        for k in range(2):
            f_copy(part, k).wait_send()
            w_copy(part, k).wait_send()
    for copy in x_copies + y_copies + z_copies + ay_copies + ax_copies:
        copy.wait_send()


def finish(filtered, blocks, out_hbm, corr_hbm, corr, sem):
    first = pltpu.make_async_copy(filtered, out_hbm, sem.at[0])
    first.start()
    for j in range(4):
        corr[j * WIDTH:(j + 1) * WIDTH, :] = blocks[j].astype(F32).T
    second = pltpu.make_async_copy(corr, corr_hbm, sem.at[1])
    second.start()
    first.wait()
    second.wait()


def solution(mesh, sizes=(4, 4, 12)):
    ny, nx, nz = sizes
    dma = pltpu.SemaphoreType.DMA

    def body(wavefunctions, hamiltonians, connectivity, face_nodes):
        filtered, blocks = pl.pallas_call(
            lambda *refs: kernel(sizes, *refs),
            out_shape=(
                jax.ShapeDtypeStruct((NODES, WIDTH), F32),
                jax.ShapeDtypeStruct((4, WIDTH, WIDTH), BF16),
            ),
            in_specs=[pl.BlockSpec(memory_space=pltpu.HBM)] * 3,
            out_specs=(pl.BlockSpec(memory_space=pltpu.VMEM),) * 2,
            scratch_shapes=[
                pltpu.VMEM((NODES, WIDTH), BF16),
                pltpu.VMEM((NODES, NODES), BF16),
                pltpu.VMEM((1, NODES), jnp.int32),
                pltpu.VMEM((ROWS, WIDTH), BF16),
                pltpu.VMEM((ROWS, WIDTH), F32),
                pltpu.VMEM((ROWS, WIDTH), BF16),
                pltpu.VMEM((ROWS, WIDTH), BF16),
                pltpu.VMEM((4, ROWS, WIDTH), BF16),
                pltpu.VMEM((2, 2, 96, WIDTH), BF16),
                pltpu.VMEM((2, 2, 96, WIDTH), BF16),
                pltpu.VMEM((4, WIDTH, WIDTH), F32),
                pltpu.VMEM((4, WIDTH, WIDTH), BF16),
                pltpu.VMEM((nx - 1, WIDTH, WIDTH), BF16),
                pltpu.VMEM((WIDTH, WIDTH), BF16),
                pltpu.VMEM((ny - 1, WIDTH // ny, WIDTH), BF16),
                pltpu.VMEM((nz, WIDTH // ny, WIDTH), BF16),
                dma((3,)),
                dma((2, 2)), dma((2, 2)),
                pltpu.SemaphoreType.REGULAR((3, 2)),
                dma((2, 2)), dma((2, 2)), dma((2, 2)), dma((2, 2)),
                dma((nx - 1,)), dma((nx - 1,)),
                dma((ny - 1,)), dma((ny - 1,)),
                dma((nz - 1,)), dma((nz - 1,)),
                dma((ny - 1,)), dma((ny - 1,)),
                dma((nx - 1,)), dma((nx - 1,)),
            ],
            compiler_params=pltpu.CompilerParams(
                collective_id=0, has_side_effects=True, vmem_limit_bytes=40 << 20
            ),
        )(*[pltpu.with_memory_space_constraint(a, pltpu.HBM) for a in (wavefunctions, hamiltonians, connectivity)])
        return pl.pallas_call(
            finish,
            out_shape=(
                jax.ShapeDtypeStruct((NODES, WIDTH), F32),
                jax.ShapeDtypeStruct((4 * WIDTH, WIDTH), F32),
            ),
            in_specs=[pl.BlockSpec(memory_space=pltpu.VMEM)] * 2,
            out_specs=(pl.BlockSpec(memory_space=pltpu.HBM),) * 2,
            scratch_shapes=[pltpu.VMEM((4 * WIDTH, WIDTH), F32), dma((2,))],
            compiler_params=pltpu.CompilerParams(vmem_limit_bytes=16 << 20),
        )(filtered, blocks)

    return jax.shard_map(
        body,
        mesh=mesh,
        in_specs=(P("cells", "bands"), P("cells", None, None), P("cells", None), P("cells", None)),
        out_specs=(P("cells", "bands"), P(None, "bands")),
        check_vma=False,
    )
```

```python
import jax
import jax.numpy as jnp
from jax import lax
from jax.experimental import pallas as pl
from jax.experimental.pallas import tpu as pltpu
from jax.sharding import PartitionSpec as P

MESH = pl.DeviceIdType.MESH
NODES = 729
SHARED = 81
FAR = NODES - SHARED
WIDTH = 128
EARLY = 640
ROWS = 736
F32 = jnp.float32
BF16 = jnp.bfloat16


def mm(a, b):
    return jnp.dot(a, b, preferred_element_type=F32)


def kernel(
    sizes,
    v_hbm, h_hbm, conn_hbm,
    out_ref, res,
    v, h, conn, u, t, y1, filt, fall, own_twin, far_twin, face_out, face_in,
    gram_f, gram_b, rs_in, rz,
    in_sem, face_send, face_recv, near, f_send, f_recv, w_send, w_recv,
    s_send, s_recv, z_send, z_recv, g_send, g_recv,
):
    ny, nx, nz = sizes
    cells = lax.axis_index("cells")
    band = lax.axis_index("bands")
    last = ny * nx * nz - 1
    z = lax.rem(cells, nz)
    x = lax.rem(cells // nz, nx)
    y = cells // (nx * nz)
    core = lax.rem(band, 2)
    plane = band // 2
    ring = 2 * ny
    half = ny // 2
    here = plane * ny + y

    def at(yy, xx, zz):
        return (yy * nx + xx) * nz + zz

    def f_peer(offset):
        there = lax.rem(here + offset + ring, ring)
        return (at(lax.rem(there, ny), x, z), (there // ny) * 2 + core)

    def x_peer(offset):
        return (at(y, lax.rem(x + offset + nx, nx), z), band)

    def z_peer(offset):
        return (at(y, x, lax.rem(z + offset + nz, nz)), band)

    def mirror(j):
        return (y, y + 1 - 2 * lax.rem(y, 2), lax.rem(y + 2, 4), 3 - y)[j]

    def xy_peer(i, j):
        return (at(mirror(j), lax.rem(x + i, nx), z), band)

    f_peers = [f_peer(half), f_peer(-half)]
    twin = (cells, band + 1 - 2 * core)
    spans = [(i, j) for i in range(nx) for j in range(ny) if i + j]
    spans.sort(key=lambda s: -(min(s[0], nx - s[0]) + s[1]))
    z_spans = sorted(range(1, nz), key=lambda k: -min(k, nz - k))

    loads = [
        pltpu.make_async_copy(conn_hbm, conn, in_sem.at[0]),
        pltpu.make_async_copy(v_hbm, v, in_sem.at[1]),
        pltpu.make_async_copy(h_hbm.at[0], h, in_sem.at[2]),
    ]
    for load in loads:
        load.start()

    barrier = pltpu.get_barrier_semaphore()
    peers = f_peers + [twin, xy_peer(0, 1), x_peer(1), x_peer(-1), z_peer(1), z_peer(-1)]
    meetings = (
        (xy_peer(0, 1), x_peer(1), x_peer(-1), z_peer(1), z_peer(-1)),
        (x_peer(1), x_peer(-1), x_peer(2), z_peer(2), z_peer(-2)),
        (z_peer(2), z_peer(-2)),
    )

    def meet(stage):
        for slot, peer in enumerate(meetings[stage]):
            pl.semaphore_signal(near.at[stage, slot], inc=1, device_id=peer, device_id_type=MESH)

    def met(stage):
        for slot in range(len(meetings[stage])):
            pl.semaphore_wait(near.at[stage, slot], 1)

    for peer in peers:
        pl.semaphore_signal(barrier, inc=1, device_id=peer, device_id_type=MESH)

    @pl.when(cells > 0)
    def _():
        pl.semaphore_signal(barrier, inc=1, device_id=(cells - 1, band), device_id_type=MESH)

    @pl.when(cells < last)
    def _():
        pl.semaphore_signal(barrier, inc=1, device_id=(cells + 1, band), device_id_type=MESH)

    def face_copy(step, side):
        peer = (cells - 1 + 2 * side, band)
        return pltpu.make_async_remote_copy(
            face_out.at[step, side], face_in.at[step, 1 - side],
            face_send.at[step, side], face_recv.at[step, 1 - side],
            device_id=peer, device_id_type=MESH,
        )

    def send_faces(step):
        @pl.when(cells > 0)
        def _():
            face_copy(step, 0).start()

        @pl.when(cells < last)
        def _():
            face_copy(step, 1).start()

    def wait_faces(step):
        @pl.when(cells > 0)
        def _():
            face_copy(step, 1).wait_recv()

        @pl.when(cells < last)
        def _():
            face_copy(step, 0).wait_recv()

    def done_faces(step):
        @pl.when(cells > 0)
        def _():
            face_copy(step, 0).wait_send()

        @pl.when(cells < last)
        def _():
            face_copy(step, 1).wait_send()

    @pl.when(cells == 0)
    def _():
        for step in range(2):
            face_in[step, 0] = jnp.zeros(face_in.shape[2:], BF16)

    @pl.when(cells == last)
    def _():
        for step in range(2):
            face_in[step, 1] = jnp.zeros(face_in.shape[2:], BF16)

    loads[0].wait()
    order = conn[...].astype(F32)
    column = jnp.broadcast_to(order, (WIDTH, NODES)).T
    lanes = lax.broadcasted_iota(jnp.int32, (NODES, WIDTH), 1).astype(F32)
    loads[1].wait()
    total = jnp.zeros((NODES, WIDTH), F32)
    for k in range(0, NODES, WIDTH):
        width = min(WIDTH, NODES - k)
        pick = jnp.where(column == lanes + float(k), 1.0, 0.0).astype(BF16)
        total += mm(pick[:, :width], v[k:k + width, :])
    u[0:NODES, :] = total.astype(BF16)

    loads[2].wait()
    t[0:96, :] = mm(h[0:96, :], u[0:NODES, :])
    t[EARLY:NODES, :] = mm(h[EARLY:NODES, :], u[0:NODES, :])
    face_out[0, 0, 0:SHARED, :] = t[0:SHARED, :].astype(BF16)
    face_out[0, 1, 0:SHARED, :] = t[FAR:NODES, :].astype(BF16)
    want = len(peers) + jnp.where(cells > 0, 1, 0) + jnp.where(cells < last, 1, 0)
    pl.semaphore_wait(barrier, want)
    meet(0)
    send_faces(0)
    t[96:EARLY, :] = mm(h[96:EARLY, :], u[0:NODES, :])
    y1[0:NODES, :] = (0.5 * t[0:NODES, :]).astype(BF16)
    y1[0:SHARED, :] = jnp.zeros((SHARED, WIDTH), BF16)
    y1[FAR:NODES, :] = jnp.zeros((SHARED, WIDTH), BF16)
    low = t[0:SHARED, :]
    high = t[FAR:NODES, :]
    t[0:NODES, :] = mm(h[...], y1[0:NODES, :])

    wait_faces(0)
    met(0)
    meet(1)
    low1 = 0.5 * (low + face_in[0, 0, 0:SHARED, :].astype(F32))
    high1 = 0.5 * (high + face_in[0, 1, 0:SHARED, :].astype(F32))
    y1[0:WIDTH, :] = jnp.zeros((WIDTH, WIDTH), BF16)
    y1[EARLY:NODES, :] = jnp.zeros((NODES - EARLY, WIDTH), BF16)
    y1[0:SHARED, :] = low1.astype(BF16)
    y1[FAR:NODES, :] = high1.astype(BF16)

    def add_faces(lo, hi):
        t[lo:hi, :] += mm(h[lo:hi, 0:WIDTH], y1[0:WIDTH, :]) + mm(h[lo:hi, EARLY:NODES], y1[EARLY:NODES, :])

    add_faces(0, 96)
    add_faces(EARLY, NODES)
    face_out[1, 0, 0:SHARED, :] = t[0:SHARED, :].astype(BF16)
    face_out[1, 1, 0:SHARED, :] = t[FAR:NODES, :].astype(BF16)
    send_faces(1)
    add_faces(96, EARLY)

    first = jnp.where(cells == 0, jnp.float32(1.0), jnp.float32(0.0))
    t[0:NODES, :] = t[0:NODES, :] - u[0:NODES, :].astype(F32)
    filt[0:NODES, :] = t[0:NODES, :].astype(BF16)
    filt[0:SHARED, :] = (t[0:SHARED, :] * first).astype(BF16)

    def rows_of(part):
        return pl.ds(0, EARLY) if part == 0 else pl.ds(EARLY, ROWS - EARLY)

    def f_copy(part, k):
        return pltpu.make_async_remote_copy(
            filt.at[rows_of(part)], fall.at[plane, rows_of(part)],
            f_send.at[part, k], f_recv.at[part, k],
            device_id=f_peers[k], device_id_type=MESH,
        )

    for k in range(2):
        f_copy(0, k).start()

    wait_faces(1)
    t[FAR:NODES, :] += face_in[1, 1, 0:SHARED, :].astype(F32)
    filt[EARLY:NODES, :] = t[EARLY:NODES, :].astype(BF16)
    filt[NODES:ROWS, :] = jnp.zeros((ROWS - NODES, WIDTH), BF16)
    for k in range(2):
        f_copy(1, k).start()
    own_copy = pltpu.make_async_remote_copy(
        filt, own_twin, w_send.at[2], w_recv.at[2], device_id=twin, device_id_type=MESH
    )
    own_copy.start()
    met(1)
    meet(2)

    t[0:SHARED, :] += face_in[1, 0, 0:SHARED, :].astype(F32)
    rows = lax.broadcasted_iota(jnp.int32, (NODES, NODES), 0).astype(F32)
    place = jnp.where(rows == jnp.broadcast_to(order, (NODES, NODES)), 1.0, 0.0).astype(BF16)
    full = t[0:NODES, :]
    coarse = full.astype(BF16)
    fine = (full - coarse.astype(F32)).astype(BF16)
    out_ref[...] = mm(place, coarse) + mm(place, fine)

    def gram(part, left, one, two):
        for side, right in ((core, one), (1 - core, two)):
            block = lax.dot_general(left, right, (((0,), (0,)), ((), ())), preferred_element_type=F32)
            tiles = block.reshape(8, 16, WIDTH)
            gram_f[part, pl.ds(8 * side, 8)] = tiles
            gram_b[part, pl.ds(8 * side, 8)] = tiles.astype(BF16)

    mine = x * ny + y

    def s_copy(part, n):
        i, j = spans[n]
        shard = lax.rem(x + i, nx) * ny + mirror(j)
        return pltpu.make_async_remote_copy(
            gram_b.at[part, shard], rs_in.at[part, n],
            s_send.at[part, n], s_recv.at[part, n],
            device_id=xy_peer(i, j), device_id_type=MESH,
        )

    def z_copy(part, n):
        return pltpu.make_async_remote_copy(
            rz.at[part, z], rz.at[part, z],
            z_send.at[part, n], z_recv.at[part, n],
            device_id=z_peer(z_spans[n]), device_id_type=MESH,
        )

    def g_copy(part, n):
        i, j = spans[n]
        block = plane if part == 0 else 1 - plane
        return pltpu.make_async_remote_copy(
            res.at[block, mine], res.at[block, mine],
            g_send.at[part, n], g_recv.at[part, n],
            device_id=xy_peer(i, j), device_id_type=MESH,
        )

    def scatter(part):
        for n in range(len(spans)):
            s_copy(part, n).start()

    def exchange(part):
        total = gram_f[part, mine]
        for n in range(len(spans)):
            s_copy(part, n).wait_recv()
        for n in range(len(spans)):
            total += rs_in[part, n].astype(F32)
        rz[part, z] = total.astype(BF16)
        for n in range(len(z_spans)):
            z_copy(part, n).start()

    def spread(part):
        for n in range(len(z_spans)):
            z_copy(part, n).wait_recv()
        total = rz[part, 0].astype(F32)
        for k in range(1, nz):
            total += rz[part, k].astype(F32)
        res[plane if part == 0 else 1 - plane, mine] = (total / float((last + 1) * NODES)).astype(BF16)
        for n in range(len(spans)):
            g_copy(part, n).start()

    own_copy.wait_recv()
    gram(0, filt[...], filt[...], own_twin[...])
    scatter(0)

    def w_copy(part):
        return pltpu.make_async_remote_copy(
            fall.at[1 - plane, rows_of(part)], far_twin.at[rows_of(part)],
            w_send.at[part], w_recv.at[part],
            device_id=twin, device_id_type=MESH,
        )

    for part in range(2):
        for k in range(2):
            f_copy(part, k).wait_recv()
        w_copy(part).start()
    met(2)
    exchange(0)
    for part in range(2):
        w_copy(part).wait_recv()
    gram(1, fall[plane], fall[1 - plane], far_twin[...])
    scatter(1)
    exchange(1)
    spread(0)
    spread(1)
    for part in range(2):
        for n in range(len(spans)):
            g_copy(part, n).wait_recv()

    done_faces(0)
    done_faces(1)
    own_copy.wait_send()
    for part in range(2):
        w_copy(part).wait_send()
        for k in range(2):
            f_copy(part, k).wait_send()
        for n in range(len(spans)):
            s_copy(part, n).wait_send()
            g_copy(part, n).wait_send()
        for n in range(len(z_spans)):
            z_copy(part, n).wait_send()


def finish(filtered, blocks, out_hbm, corr_hbm, corr, sem):
    first = pltpu.make_async_copy(filtered, out_hbm, sem.at[0])
    first.start()
    for j in range(4):
        corr[j * WIDTH:(j + 1) * WIDTH, :] = blocks[j].astype(F32).T
    second = pltpu.make_async_copy(corr, corr_hbm, sem.at[1])
    second.start()
    first.wait()
    second.wait()


def solution(mesh, sizes=(4, 4, 12)):
    ny, nx, nz = sizes
    dma = pltpu.SemaphoreType.DMA

    def body(wavefunctions, hamiltonians, connectivity, face_nodes):
        filtered, blocks = pl.pallas_call(
            lambda *refs: kernel(sizes, *refs),
            out_shape=(
                jax.ShapeDtypeStruct((NODES, WIDTH), F32),
                jax.ShapeDtypeStruct((2, 16, 16, WIDTH), BF16),
            ),
            in_specs=[pl.BlockSpec(memory_space=pltpu.HBM)] * 3,
            out_specs=(pl.BlockSpec(memory_space=pltpu.VMEM),) * 2,
            scratch_shapes=[
                pltpu.VMEM((NODES, WIDTH), BF16),
                pltpu.VMEM((NODES, NODES), BF16),
                pltpu.VMEM((1, NODES), jnp.int32),
                pltpu.VMEM((ROWS, WIDTH), BF16),
                pltpu.VMEM((ROWS, WIDTH), F32),
                pltpu.VMEM((ROWS, WIDTH), BF16),
                pltpu.VMEM((ROWS, WIDTH), BF16),
                pltpu.VMEM((2, ROWS, WIDTH), BF16),
                pltpu.VMEM((ROWS, WIDTH), BF16),
                pltpu.VMEM((ROWS, WIDTH), BF16),
                pltpu.VMEM((2, 2, 96, WIDTH), BF16),
                pltpu.VMEM((2, 2, 96, WIDTH), BF16),
                pltpu.VMEM((2, 16, 16, WIDTH), F32),
                pltpu.VMEM((2, 16, 16, WIDTH), BF16),
                pltpu.VMEM((2, nx * ny - 1, 16, WIDTH), BF16),
                pltpu.VMEM((2, nz, 16, WIDTH), BF16),
                dma((3,)),
                dma((2, 2)), dma((2, 2)),
                pltpu.SemaphoreType.REGULAR((3, 5)),
                dma((2, 2)), dma((2, 2)), dma((3,)), dma((3,)),
                dma((2, nx * ny - 1)), dma((2, nx * ny - 1)),
                dma((2, nz - 1)), dma((2, nz - 1)),
                dma((2, nx * ny - 1)), dma((2, nx * ny - 1)),
            ],
            compiler_params=pltpu.CompilerParams(
                collective_id=0, has_side_effects=True, vmem_limit_bytes=40 << 20
            ),
        )(*[pltpu.with_memory_space_constraint(a, pltpu.HBM) for a in (wavefunctions, hamiltonians, connectivity)])
        return pl.pallas_call(
            finish,
            out_shape=(
                jax.ShapeDtypeStruct((NODES, WIDTH), F32),
                jax.ShapeDtypeStruct((4 * WIDTH, WIDTH), F32),
            ),
            in_specs=[pl.BlockSpec(memory_space=pltpu.VMEM)] * 2,
            out_specs=(pl.BlockSpec(memory_space=pltpu.HBM),) * 2,
            scratch_shapes=[pltpu.VMEM((4 * WIDTH, WIDTH), F32), dma((2,))],
            compiler_params=pltpu.CompilerParams(vmem_limit_bytes=16 << 20),
        )(filtered, blocks.reshape(4, WIDTH, WIDTH))

    return jax.shard_map(
        body,
        mesh=mesh,
        in_specs=(P("cells", "bands"), P("cells", None, None), P("cells", None), P("cells", None)),
        out_specs=(P("cells", "bands"), P(None, "bands")),
        check_vma=False,
    )
```

```python
import jax
import jax.numpy as jnp
from jax import lax
from jax.experimental import pallas as pl
from jax.experimental.pallas import tpu as pltpu
from jax.sharding import PartitionSpec as P

MESH = pl.DeviceIdType.MESH
NODES = 729
SHARED = 81
FAR = NODES - SHARED
WIDTH = 128
EARLY = 640
LOW = 80
ROWS = 736
F32 = jnp.float32
BF16 = jnp.bfloat16


def mm(a, b):
    return jnp.dot(a, b, preferred_element_type=F32)


def kernel(
    sizes,
    v_hbm, h_hbm, conn_hbm,
    out_ref, res,
    v, h, conn, u, t, y1, filt, fall, own_twin, far_twin, face_out, face_in,
    gram_f, gram_b, rs_in, rz,
    in_sem, face_send, face_recv, near, f_send, f_recv, w_send, w_recv,
    s_send, s_recv, z_send, z_recv, g_send, g_recv,
):
    ny, nx, nz = sizes
    cells = lax.axis_index("cells")
    band = lax.axis_index("bands")
    last = ny * nx * nz - 1
    z = lax.rem(cells, nz)
    x = lax.rem(cells // nz, nx)
    y = cells // (nx * nz)
    core = lax.rem(band, 2)
    plane = band // 2
    ring = 2 * ny
    half = ny // 2
    here = plane * ny + y

    def at(yy, xx, zz):
        return (yy * nx + xx) * nz + zz

    def f_peer(offset):
        there = lax.rem(here + offset + ring, ring)
        return (at(lax.rem(there, ny), x, z), (there // ny) * 2 + core)

    def x_peer(offset):
        return (at(y, lax.rem(x + offset + nx, nx), z), band)

    def z_peer(offset):
        return (at(y, x, lax.rem(z + offset + nz, nz)), band)

    def mirror(j):
        return (y, y + 1 - 2 * lax.rem(y, 2), lax.rem(y + 2, 4), 3 - y)[j]

    def xy_peer(i, j):
        return (at(mirror(j), lax.rem(x + i, nx), z), band)

    f_peers = [f_peer(half), f_peer(-half)]
    twin = (cells, band + 1 - 2 * core)
    spans = [(i, j) for i in range(nx) for j in range(ny) if i + j]
    spans.sort(key=lambda s: -(min(s[0], nx - s[0]) + s[1]))
    z_spans = sorted(range(1, nz), key=lambda k: -min(k, nz - k))

    loads = [
        pltpu.make_async_copy(conn_hbm, conn, in_sem.at[0]),
        pltpu.make_async_copy(v_hbm, v, in_sem.at[1]),
        pltpu.make_async_copy(h_hbm.at[0, pl.ds(0, 96)], h.at[pl.ds(0, 96)], in_sem.at[2]),
        pltpu.make_async_copy(
            h_hbm.at[0, pl.ds(EARLY, NODES - EARLY)], h.at[pl.ds(EARLY, NODES - EARLY)], in_sem.at[3]
        ),
        pltpu.make_async_copy(h_hbm.at[0, pl.ds(96, EARLY - 96)], h.at[pl.ds(96, EARLY - 96)], in_sem.at[4]),
    ]
    for load in loads:
        load.start()

    barrier = pltpu.get_barrier_semaphore()
    cross = (at(lax.rem(y + half, ny), x, z), (1 - plane) * 2 + 1 - core)
    peers = f_peers + [cross, twin, xy_peer(0, 1), x_peer(1), x_peer(-1), z_peer(1), z_peer(-1)]
    meetings = (
        (xy_peer(0, 1), x_peer(1), x_peer(-1), z_peer(1), z_peer(-1)),
        (x_peer(1), x_peer(-1), x_peer(2), z_peer(2), z_peer(-2)),
        (z_peer(2), z_peer(-2)),
    )

    def meet(stage):
        for slot, peer in enumerate(meetings[stage]):
            pl.semaphore_signal(near.at[stage, slot], inc=1, device_id=peer, device_id_type=MESH)

    def met(stage):
        for slot in range(len(meetings[stage])):
            pl.semaphore_wait(near.at[stage, slot], 1)

    for peer in peers:
        pl.semaphore_signal(barrier, inc=1, device_id=peer, device_id_type=MESH)

    @pl.when(cells > 0)
    def _():
        pl.semaphore_signal(barrier, inc=1, device_id=(cells - 1, band), device_id_type=MESH)

    @pl.when(cells < last)
    def _():
        pl.semaphore_signal(barrier, inc=1, device_id=(cells + 1, band), device_id_type=MESH)

    def face_copy(step, side):
        peer = (cells - 1 + 2 * side, band)
        return pltpu.make_async_remote_copy(
            face_out.at[step, side], face_in.at[step, 1 - side],
            face_send.at[step, side], face_recv.at[step, 1 - side],
            device_id=peer, device_id_type=MESH,
        )

    def send_faces(step):
        @pl.when(cells > 0)
        def _():
            face_copy(step, 0).start()

        @pl.when(cells < last)
        def _():
            face_copy(step, 1).start()

    def wait_faces(step):
        @pl.when(cells > 0)
        def _():
            face_copy(step, 1).wait_recv()

        @pl.when(cells < last)
        def _():
            face_copy(step, 0).wait_recv()

    def done_faces(step):
        @pl.when(cells > 0)
        def _():
            face_copy(step, 0).wait_send()

        @pl.when(cells < last)
        def _():
            face_copy(step, 1).wait_send()

    @pl.when(cells == 0)
    def _():
        for step in range(2):
            face_in[step, 0] = jnp.zeros(face_in.shape[2:], BF16)

    @pl.when(cells == last)
    def _():
        for step in range(2):
            face_in[step, 1] = jnp.zeros(face_in.shape[2:], BF16)

    far_first = at(lax.rem(y + half, ny), x, z) == 0

    @pl.when(jnp.logical_not(far_first))
    def _():
        fall[0, 0:LOW, :] = jnp.zeros((LOW, WIDTH), BF16)
        fall[1, 0:LOW, :] = jnp.zeros((LOW, WIDTH), BF16)
        far_twin[0:LOW, :] = jnp.zeros((LOW, WIDTH), BF16)

    loads[0].wait()
    order = conn[...].astype(F32)
    column = jnp.broadcast_to(order, (WIDTH, NODES)).T
    lanes = lax.broadcasted_iota(jnp.int32, (NODES, WIDTH), 1).astype(F32)
    loads[1].wait()
    total = jnp.zeros((NODES, WIDTH), F32)
    for k in range(0, NODES, WIDTH):
        width = min(WIDTH, NODES - k)
        pick = jnp.where(column == lanes + float(k), 1.0, 0.0).astype(BF16)
        total += mm(pick[:, :width], v[k:k + width, :])
    u[0:NODES, :] = total.astype(BF16)

    loads[2].wait()
    loads[3].wait()
    t[0:96, :] = mm(h[0:96, :], u[0:NODES, :])
    t[EARLY:NODES, :] = mm(h[EARLY:NODES, :], u[0:NODES, :])
    face_out[0, 0, 0:SHARED, :] = t[0:SHARED, :].astype(BF16)
    face_out[0, 1, 0:SHARED, :] = t[FAR:NODES, :].astype(BF16)
    want = len(peers) + jnp.where(cells > 0, 1, 0) + jnp.where(cells < last, 1, 0)
    pl.semaphore_wait(barrier, want)
    meet(0)
    send_faces(0)
    loads[4].wait()
    t[96:EARLY, :] = mm(h[96:EARLY, :], u[0:NODES, :])
    y1[0:NODES, :] = (0.5 * t[0:NODES, :]).astype(BF16)
    y1[0:SHARED, :] = jnp.zeros((SHARED, WIDTH), BF16)
    y1[FAR:NODES, :] = jnp.zeros((SHARED, WIDTH), BF16)
    low = t[0:SHARED, :]
    high = t[FAR:NODES, :]
    t[0:NODES, :] = mm(h[...], y1[0:NODES, :])

    wait_faces(0)
    met(0)
    meet(1)
    low1 = 0.5 * (low + face_in[0, 0, 0:SHARED, :].astype(F32))
    high1 = 0.5 * (high + face_in[0, 1, 0:SHARED, :].astype(F32))
    y1[0:WIDTH, :] = jnp.zeros((WIDTH, WIDTH), BF16)
    y1[EARLY:NODES, :] = jnp.zeros((NODES - EARLY, WIDTH), BF16)
    y1[0:SHARED, :] = low1.astype(BF16)
    y1[FAR:NODES, :] = high1.astype(BF16)

    def add_faces(lo, hi):
        t[lo:hi, :] += mm(h[lo:hi, 0:WIDTH], y1[0:WIDTH, :]) + mm(h[lo:hi, EARLY:NODES], y1[EARLY:NODES, :])

    add_faces(0, 96)
    add_faces(EARLY, NODES)
    face_out[1, 0, 0:SHARED, :] = t[0:SHARED, :].astype(BF16)
    face_out[1, 1, 0:SHARED, :] = t[FAR:NODES, :].astype(BF16)
    send_faces(1)
    add_faces(96, EARLY)

    first = jnp.where(cells == 0, jnp.float32(1.0), jnp.float32(0.0))
    t[0:NODES, :] = t[0:NODES, :] - u[0:NODES, :].astype(F32)
    filt[0:NODES, :] = t[0:NODES, :].astype(BF16)
    filt[0:SHARED, :] = (t[0:SHARED, :] * first).astype(BF16)

    def rows_of(part):
        return (pl.ds(LOW, EARLY - LOW), pl.ds(EARLY, ROWS - EARLY), pl.ds(0, LOW))[part]

    def f_copy(part, k):
        return pltpu.make_async_remote_copy(
            filt.at[rows_of(part)], fall.at[plane, rows_of(part)],
            f_send.at[part, k], f_recv.at[part, k],
            device_id=f_peers[k], device_id_type=MESH,
        )

    for k in range(2):
        f_copy(0, k).start()

    @pl.when(cells == 0)
    def _():
        for k in range(2):
            f_copy(2, k).start()

    cross_copy = pltpu.make_async_remote_copy(
        filt.at[rows_of(1)], far_twin.at[rows_of(1)],
        w_send.at[1], w_recv.at[1], device_id=cross, device_id_type=MESH,
    )

    wait_faces(1)
    t[FAR:NODES, :] += face_in[1, 1, 0:SHARED, :].astype(F32)
    filt[EARLY:NODES, :] = t[EARLY:NODES, :].astype(BF16)
    filt[NODES:ROWS, :] = jnp.zeros((ROWS - NODES, WIDTH), BF16)
    for k in range(2):
        f_copy(1, k).start()
    cross_copy.start()
    own_copy = pltpu.make_async_remote_copy(
        filt, own_twin, w_send.at[3], w_recv.at[3], device_id=twin, device_id_type=MESH
    )
    own_copy.start()
    met(1)
    meet(2)

    t[0:SHARED, :] += face_in[1, 0, 0:SHARED, :].astype(F32)
    rows = lax.broadcasted_iota(jnp.int32, (NODES, NODES), 0).astype(F32)
    place = jnp.where(rows == jnp.broadcast_to(order, (NODES, NODES)), 1.0, 0.0).astype(BF16)
    full = t[0:NODES, :]
    coarse = full.astype(BF16)
    fine = (full - coarse.astype(F32)).astype(BF16)
    out_ref[...] = mm(place, coarse) + mm(place, fine)

    def gram(part, left, one, two):
        for side, right in ((core, one), (1 - core, two)):
            block = lax.dot_general(left, right, (((0,), (0,)), ((), ())), preferred_element_type=F32)
            tiles = block.reshape(8, 16, WIDTH)
            gram_f[part, pl.ds(8 * side, 8)] = tiles
            gram_b[part, pl.ds(8 * side, 8)] = tiles.astype(BF16)

    mine = x * ny + y

    def s_copy(part, n):
        i, j = spans[n]
        shard = lax.rem(x + i, nx) * ny + mirror(j)
        return pltpu.make_async_remote_copy(
            gram_b.at[part, shard], rs_in.at[part, n],
            s_send.at[part], s_recv.at[part],
            device_id=xy_peer(i, j), device_id_type=MESH,
        )

    def z_copy(part, n):
        return pltpu.make_async_remote_copy(
            rz.at[part, z], rz.at[part, z],
            z_send.at[part], z_recv.at[part],
            device_id=z_peer(z_spans[n]), device_id_type=MESH,
        )

    def g_copy(part, n):
        i, j = spans[n]
        block = plane if part == 0 else 1 - plane
        return pltpu.make_async_remote_copy(
            res.at[block, mine], res.at[block, mine],
            g_send.at[part], g_recv.at[part],
            device_id=xy_peer(i, j), device_id_type=MESH,
        )

    def all_of(ref, send, recv):
        return pltpu.make_async_remote_copy(ref, ref, send, recv, device_id=twin, device_id_type=MESH)

    def s_all(part):
        return all_of(rs_in.at[part], s_send.at[part], s_recv.at[part])

    def z_all(part):
        return all_of(rz.at[part, pl.ds(0, nz - 1)], z_send.at[part], z_recv.at[part])

    def g_all(part):
        return all_of(rs_in.at[part], g_send.at[part], g_recv.at[part])

    def scatter(part):
        for n in range(len(spans)):
            s_copy(part, n).start()

    def exchange(part):
        total = gram_f[part, mine]
        s_all(part).wait_recv()
        for n in range(len(spans)):
            total += rs_in[part, n].astype(F32)
        rz[part, z] = total.astype(BF16)
        for n in range(len(z_spans)):
            z_copy(part, n).start()

    def spread(part):
        z_all(part).wait_recv()
        total = rz[part, 0].astype(F32)
        for k in range(1, nz):
            total += rz[part, k].astype(F32)
        res[plane if part == 0 else 1 - plane, mine] = (total / float((last + 1) * NODES)).astype(BF16)
        for n in range(len(spans)):
            g_copy(part, n).start()

    own_copy.wait_recv()
    gram(0, filt[...], filt[...], own_twin[...])
    scatter(0)

    def w_copy(part):
        return pltpu.make_async_remote_copy(
            fall.at[1 - plane, rows_of(part)], far_twin.at[rows_of(part)],
            w_send.at[part], w_recv.at[part],
            device_id=twin, device_id_type=MESH,
        )

    for k in range(2):
        f_copy(0, k).wait_recv()
    w_copy(0).start()

    @pl.when(far_first)
    def _():
        for k in range(2):
            f_copy(2, k).wait_recv()
        w_copy(2).start()
        w_copy(2).wait_recv()

    for k in range(2):
        f_copy(1, k).wait_recv()
    cross_copy.wait_recv()
    w_copy(0).wait_recv()
    gram(1, fall[plane], fall[1 - plane], far_twin[...])
    scatter(1)
    met(2)
    exchange(0)
    exchange(1)
    spread(0)
    spread(1)
    for part in range(2):
        g_all(part).wait_recv()

    done_faces(0)
    done_faces(1)
    own_copy.wait_send()
    cross_copy.wait_send()
    w_copy(0).wait_send()

    @pl.when(far_first)
    def _():
        w_copy(2).wait_send()

    @pl.when(cells == 0)
    def _():
        for k in range(2):
            f_copy(2, k).wait_send()

    for part in range(2):
        for k in range(2):
            f_copy(part, k).wait_send()
        s_all(part).wait_send()
        z_all(part).wait_send()
        g_all(part).wait_send()


def finish(filtered, blocks, out_hbm, corr_hbm, corr, sem):
    first = pltpu.make_async_copy(filtered, out_hbm, sem.at[0])
    first.start()
    for j in range(4):
        corr[j * WIDTH:(j + 1) * WIDTH, :] = blocks[j].astype(F32).T
    second = pltpu.make_async_copy(corr, corr_hbm, sem.at[1])
    second.start()
    first.wait()
    second.wait()


def solution(mesh, sizes=(4, 4, 12)):
    ny, nx, nz = sizes
    dma = pltpu.SemaphoreType.DMA

    def body(wavefunctions, hamiltonians, connectivity, face_nodes):
        filtered, blocks = pl.pallas_call(
            lambda *refs: kernel(sizes, *refs),
            out_shape=(
                jax.ShapeDtypeStruct((NODES, WIDTH), F32),
                jax.ShapeDtypeStruct((2, 16, 16, WIDTH), BF16),
            ),
            in_specs=[pl.BlockSpec(memory_space=pltpu.HBM)] * 3,
            out_specs=(pl.BlockSpec(memory_space=pltpu.VMEM),) * 2,
            scratch_shapes=[
                pltpu.VMEM((NODES, WIDTH), BF16),
                pltpu.VMEM((NODES, NODES), BF16),
                pltpu.VMEM((1, NODES), jnp.int32),
                pltpu.VMEM((ROWS, WIDTH), BF16),
                pltpu.VMEM((ROWS, WIDTH), F32),
                pltpu.VMEM((ROWS, WIDTH), BF16),
                pltpu.VMEM((ROWS, WIDTH), BF16),
                pltpu.VMEM((2, ROWS, WIDTH), BF16),
                pltpu.VMEM((ROWS, WIDTH), BF16),
                pltpu.VMEM((ROWS, WIDTH), BF16),
                pltpu.VMEM((2, 2, 96, WIDTH), BF16),
                pltpu.VMEM((2, 2, 96, WIDTH), BF16),
                pltpu.VMEM((2, 16, 16, WIDTH), F32),
                pltpu.VMEM((2, 16, 16, WIDTH), BF16),
                pltpu.VMEM((2, nx * ny - 1, 16, WIDTH), BF16),
                pltpu.VMEM((2, nz, 16, WIDTH), BF16),
                dma((5,)),
                dma((2, 2)), dma((2, 2)),
                pltpu.SemaphoreType.REGULAR((3, 5)),
                dma((3, 2)), dma((3, 2)), dma((4,)), dma((4,)),
                dma((2,)), dma((2,)), dma((2,)), dma((2,)), dma((2,)), dma((2,)),
            ],
            compiler_params=pltpu.CompilerParams(
                collective_id=0, has_side_effects=True, vmem_limit_bytes=40 << 20
            ),
        )(*[pltpu.with_memory_space_constraint(a, pltpu.HBM) for a in (wavefunctions, hamiltonians, connectivity)])
        return pl.pallas_call(
            finish,
            out_shape=(
                jax.ShapeDtypeStruct((NODES, WIDTH), F32),
                jax.ShapeDtypeStruct((4 * WIDTH, WIDTH), F32),
            ),
            in_specs=[pl.BlockSpec(memory_space=pltpu.VMEM)] * 2,
            out_specs=(pl.BlockSpec(memory_space=pltpu.HBM),) * 2,
            scratch_shapes=[pltpu.VMEM((4 * WIDTH, WIDTH), F32), dma((2,))],
            compiler_params=pltpu.CompilerParams(vmem_limit_bytes=16 << 20),
        )(filtered, blocks.reshape(4, WIDTH, WIDTH))

    return jax.shard_map(
        body,
        mesh=mesh,
        in_specs=(P("cells", "bands"), P("cells", None, None), P("cells", None), P("cells", None)),
        out_specs=(P("cells", "bands"), P(None, "bands")),
        check_vma=False,
    )
```

```python
import jax
import jax.numpy as jnp
from jax import lax
from jax.experimental import pallas as pl
from jax.experimental.pallas import tpu as pltpu
from jax.sharding import PartitionSpec as P

MESH = pl.DeviceIdType.MESH
NODES = 729
SHARED = 81
FAR = NODES - SHARED
WIDTH = 128
EARLY = 640
LOW = 80
CUT = 400
ROWS = 736
F32 = jnp.float32
BF16 = jnp.bfloat16


def mm(a, b):
    return jnp.dot(a, b, preferred_element_type=F32)


def kernel(
    sizes,
    v_hbm, h_hbm, conn_hbm,
    out_ref, res,
    v, h, conn, u, t, y1, filt, whole, fall, own_twin, far_twin, late, face_out, face_in, next_in,
    gram_f, gram_b, rs_in, rz,
    in_sem, face_send, face_recv, near, link, next_send, next_recv, f_send, f_recv, w_send, w_recv,
    s_send, s_recv, z_send, z_recv, g_send, g_recv,
):
    ny, nx, nz = sizes
    cells = lax.axis_index("cells")
    band = lax.axis_index("bands")
    last = ny * nx * nz - 1
    z = lax.rem(cells, nz)
    x = lax.rem(cells // nz, nx)
    y = cells // (nx * nz)
    core = lax.rem(band, 2)
    plane = band // 2
    ring = 2 * ny
    half = ny // 2
    here = plane * ny + y

    def at(yy, xx, zz):
        return (yy * nx + xx) * nz + zz

    def f_peer(offset):
        there = lax.rem(here + offset + ring, ring)
        return (at(lax.rem(there, ny), x, z), (there // ny) * 2 + core)

    def x_peer(offset):
        return (at(y, lax.rem(x + offset + nx, nx), z), band)

    def z_peer(offset):
        return (at(y, x, lax.rem(z + offset + nz, nz)), band)

    def mirror(j):
        return (y, y + 1 - 2 * lax.rem(y, 2), lax.rem(y + 2, 4), 3 - y)[j]

    def xy_peer(i, j):
        return (at(mirror(j), lax.rem(x + i, nx), z), band)

    f_peers = [f_peer(half), f_peer(-half)]
    twin = (cells, band + 1 - 2 * core)
    spans = [(i, j) for i in range(nx) for j in range(ny) if i + j]
    spans.sort(key=lambda s: -(min(s[0], nx - s[0]) + s[1]))
    z_spans = sorted(range(1, nz), key=lambda k: -min(k, nz - k))

    loads = [
        pltpu.make_async_copy(conn_hbm, conn, in_sem.at[0]),
        pltpu.make_async_copy(v_hbm, v, in_sem.at[1]),
        pltpu.make_async_copy(h_hbm.at[0, pl.ds(0, 96)], h.at[pl.ds(0, 96)], in_sem.at[2]),
        pltpu.make_async_copy(
            h_hbm.at[0, pl.ds(EARLY, NODES - EARLY)], h.at[pl.ds(EARLY, NODES - EARLY)], in_sem.at[3]
        ),
        pltpu.make_async_copy(h_hbm.at[0, pl.ds(96, EARLY - 96)], h.at[pl.ds(96, EARLY - 96)], in_sem.at[4]),
    ]
    for load in loads:
        load.start()

    barrier = pltpu.get_barrier_semaphore()
    cross = (at(lax.rem(y + half, ny), x, z), (1 - plane) * 2 + 1 - core)
    peers = f_peers + [cross, twin, xy_peer(0, 1), x_peer(1), x_peer(-1), z_peer(1), z_peer(-1)]
    meetings = (
        (xy_peer(0, 1), x_peer(1), x_peer(-1), z_peer(1), z_peer(-1)),
        (x_peer(1), x_peer(-1), x_peer(2), z_peer(2), z_peer(-2)),
        (z_peer(2), z_peer(-2)),
    )

    def meet(stage):
        for peer in meetings[stage]:
            pl.semaphore_signal(near.at[stage], inc=1, device_id=peer, device_id_type=MESH)

    def met(stage):
        pl.semaphore_wait(near.at[stage], len(meetings[stage]))

    for peer in peers:
        pl.semaphore_signal(barrier, inc=1, device_id=peer, device_id_type=MESH)

    @pl.when(cells > 0)
    def _():
        pl.semaphore_signal(barrier, inc=1, device_id=(cells - 1, band), device_id_type=MESH)

    @pl.when(cells < last)
    def _():
        pl.semaphore_signal(barrier, inc=1, device_id=(cells + 1, band), device_id_type=MESH)

    def face_copy(step, side):
        peer = (cells - 1 + 2 * side, band)
        return pltpu.make_async_remote_copy(
            face_out.at[step, side], face_in.at[step, 1 - side],
            face_send.at[step, side], face_recv.at[step, 1 - side],
            device_id=peer, device_id_type=MESH,
        )

    def send_faces(step):
        @pl.when(cells > 0)
        def _():
            face_copy(step, 0).start()

        @pl.when(cells < last)
        def _():
            face_copy(step, 1).start()

    def wait_faces(step):
        @pl.when(cells > 0)
        def _():
            face_copy(step, 1).wait_recv()

        @pl.when(cells < last)
        def _():
            face_copy(step, 0).wait_recv()

    def done_faces(step):
        @pl.when(cells > 0)
        def _():
            face_copy(step, 0).wait_send()

        @pl.when(cells < last)
        def _():
            face_copy(step, 1).wait_send()

    @pl.when(cells == 0)
    def _():
        for step in range(2):
            face_in[step, 0] = jnp.zeros(face_in.shape[2:], BF16)

    @pl.when(cells == last)
    def _():
        for step in range(2):
            face_in[step, 1] = jnp.zeros(face_in.shape[2:], BF16)

    far = at(lax.rem(y + half, ny), x, z)
    far_first = far == 0
    far_last = far == last

    @pl.when(far_last)
    def _():
        next_in[...] = jnp.zeros(next_in.shape, BF16)

    @pl.when(jnp.logical_not(far_first))
    def _():
        fall[0, 0:LOW, :] = jnp.zeros((LOW, WIDTH), BF16)
        fall[1, 0:LOW, :] = jnp.zeros((LOW, WIDTH), BF16)
        far_twin[0:LOW, :] = jnp.zeros((LOW, WIDTH), BF16)

    loads[0].wait()
    order = conn[...].astype(F32)
    column = jnp.broadcast_to(order, (WIDTH, NODES)).T
    lanes = lax.broadcasted_iota(jnp.int32, (NODES, WIDTH), 1).astype(F32)
    loads[1].wait()
    total = jnp.zeros((NODES, WIDTH), F32)
    for k in range(0, NODES, WIDTH):
        width = min(WIDTH, NODES - k)
        pick = jnp.where(column == lanes + float(k), 1.0, 0.0).astype(BF16)
        total += mm(pick[:, :width], v[k:k + width, :])
    u[0:NODES, :] = total.astype(BF16)

    loads[2].wait()
    loads[3].wait()
    t[0:96, :] = mm(h[0:96, :], u[0:NODES, :])
    t[EARLY:NODES, :] = mm(h[EARLY:NODES, :], u[0:NODES, :])
    face_out[0, 0, 0:SHARED, :] = t[0:SHARED, :].astype(BF16)
    face_out[0, 1, 0:SHARED, :] = t[FAR:NODES, :].astype(BF16)
    want = len(peers) + jnp.where(cells > 0, 1, 0) + jnp.where(cells < last, 1, 0)
    pl.semaphore_wait(barrier, want)
    meet(0)

    @pl.when(cells < last)
    def _():
        pl.semaphore_signal(link, inc=1, device_id=(cells + 1, band), device_id_type=MESH)

    send_faces(0)
    loads[4].wait()
    t[96:EARLY, :] = mm(h[96:EARLY, :], u[0:NODES, :])
    y1[0:NODES, :] = (0.5 * t[0:NODES, :]).astype(BF16)
    y1[0:SHARED, :] = jnp.zeros((SHARED, WIDTH), BF16)
    y1[FAR:NODES, :] = jnp.zeros((SHARED, WIDTH), BF16)
    low = t[0:SHARED, :]
    high = t[FAR:NODES, :]
    t[0:NODES, :] = mm(h[...], y1[0:NODES, :])

    wait_faces(0)
    met(0)

    @pl.when(cells > 0)
    def _():
        pl.semaphore_wait(link, 1)

    meet(1)
    low1 = 0.5 * (low + face_in[0, 0, 0:SHARED, :].astype(F32))
    high1 = 0.5 * (high + face_in[0, 1, 0:SHARED, :].astype(F32))
    y1[0:WIDTH, :] = jnp.zeros((WIDTH, WIDTH), BF16)
    y1[EARLY:NODES, :] = jnp.zeros((NODES - EARLY, WIDTH), BF16)
    y1[0:SHARED, :] = low1.astype(BF16)
    y1[FAR:NODES, :] = high1.astype(BF16)

    def add_faces(lo, hi):
        t[lo:hi, :] += mm(h[lo:hi, 0:WIDTH], y1[0:WIDTH, :]) + mm(h[lo:hi, EARLY:NODES], y1[EARLY:NODES, :])

    add_faces(0, 96)
    add_faces(EARLY, NODES)
    face_out[1, 0, 0:SHARED, :] = t[0:SHARED, :].astype(BF16)
    face_out[1, 1, 0:SHARED, :] = t[FAR:NODES, :].astype(BF16)
    send_faces(1)
    prior = lax.rem(cells + last, last + 1)
    prior_z, prior_x, prior_y = lax.rem(prior, nz), lax.rem(prior // nz, nx), prior // (nx * nz)

    def next_copy(k):
        if k < 2:
            there = lax.rem(plane * ny + prior_y + half * (1 - 2 * k) + ring, ring)
            peer = (at(lax.rem(there, ny), prior_x, prior_z), (there // ny) * 2 + core)
            slot = plane
        else:
            peer = (at(lax.rem(prior_y + half, ny), prior_x, prior_z), (1 - plane) * 2 + 1 - core)
            slot = 2
        return pltpu.make_async_remote_copy(
            face_out.at[1, 0], next_in.at[slot],
            next_send.at[k], next_recv.at[k],
            device_id=peer, device_id_type=MESH,
        )

    @pl.when(cells > 0)
    def _():
        for k in range(3):
            next_copy(k).start()

    add_faces(96, EARLY)

    first = jnp.where(cells == 0, jnp.float32(1.0), jnp.float32(0.0))
    t[0:NODES, :] = t[0:NODES, :] - u[0:NODES, :].astype(F32)
    filt[0:NODES, :] = t[0:NODES, :].astype(BF16)
    filt[0:SHARED, :] = (t[0:SHARED, :] * first).astype(BF16)
    filt[NODES:ROWS, :] = jnp.zeros((ROWS - NODES, WIDTH), BF16)

    def rows_of(part):
        return (pl.ds(LOW, CUT - LOW), pl.ds(CUT, ROWS - CUT), pl.ds(0, LOW))[part]

    def f_copy(part, k):
        return pltpu.make_async_remote_copy(
            filt.at[rows_of(part)], fall.at[plane, rows_of(part)],
            f_send.at[part, k], f_recv.at[part, k],
            device_id=f_peers[k], device_id_type=MESH,
        )

    for part in range(2):
        for k in range(2):
            f_copy(part, k).start()

    @pl.when(cells == 0)
    def _():
        for k in range(2):
            f_copy(2, k).start()

    wait_faces(1)
    whole[0:EARLY, :] = filt[0:EARLY, :]
    t[0:SHARED, :] += face_in[1, 0, 0:SHARED, :].astype(F32)
    t[FAR:NODES, :] += face_in[1, 1, 0:SHARED, :].astype(F32)
    whole[EARLY:NODES, :] = t[EARLY:NODES, :].astype(BF16)
    whole[NODES:ROWS, :] = jnp.zeros((ROWS - NODES, WIDTH), BF16)
    own_copy = pltpu.make_async_remote_copy(
        whole, own_twin, w_send.at[3], w_recv.at[3], device_id=twin, device_id_type=MESH
    )
    own_copy.start()
    met(1)
    meet(2)

    def gram(part, left, one, two):
        for side, right in ((core, one), (1 - core, two)):
            block = sum(
                lax.dot_general(a, b, (((0,), (0,)), ((), ())), preferred_element_type=F32)
                for a, b in zip(left, right)
            )
            tiles = block.reshape(8, 16, WIDTH)
            gram_f[part, pl.ds(8 * side, 8)] = tiles
            gram_b[part, pl.ds(8 * side, 8)] = tiles.astype(BF16)

    mine = x * ny + y

    def s_copy(part, n):
        i, j = spans[n]
        shard = lax.rem(x + i, nx) * ny + mirror(j)
        return pltpu.make_async_remote_copy(
            gram_b.at[part, shard], rs_in.at[part, n],
            s_send.at[part], s_recv.at[part],
            device_id=xy_peer(i, j), device_id_type=MESH,
        )

    def z_copy(part, n):
        return pltpu.make_async_remote_copy(
            rz.at[part, z], rz.at[part, z],
            z_send.at[part], z_recv.at[part],
            device_id=z_peer(z_spans[n]), device_id_type=MESH,
        )

    def g_copy(part, n):
        i, j = spans[n]
        block = plane if part == 0 else 1 - plane
        return pltpu.make_async_remote_copy(
            res.at[block, mine], res.at[block, mine],
            g_send.at[part], g_recv.at[part],
            device_id=xy_peer(i, j), device_id_type=MESH,
        )

    def all_of(ref, send, recv):
        return pltpu.make_async_remote_copy(ref, ref, send, recv, device_id=twin, device_id_type=MESH)

    def s_all(part):
        return all_of(rs_in.at[part], s_send.at[part], s_recv.at[part])

    def z_all(part):
        return all_of(rz.at[part, pl.ds(0, nz - 1)], z_send.at[part], z_recv.at[part])

    def g_all(part):
        return all_of(rs_in.at[part], g_send.at[part], g_recv.at[part])

    def scatter(part):
        for n in range(len(spans)):
            s_copy(part, n).start()

    def exchange(part):
        total = gram_f[part, mine]
        s_all(part).wait_recv()
        for n in range(len(spans)):
            total += rs_in[part, n].astype(F32)
        rz[part, z] = total.astype(BF16)
        for n in range(len(z_spans)):
            z_copy(part, n).start()

    def spread(part):
        z_all(part).wait_recv()
        total = rz[part, 0].astype(F32)
        for k in range(1, nz):
            total += rz[part, k].astype(F32)
        res[plane if part == 0 else 1 - plane, mine] = (total / float((last + 1) * NODES)).astype(BF16)
        for n in range(len(spans)):
            g_copy(part, n).start()

    def w_copy(part):
        return pltpu.make_async_remote_copy(
            fall.at[1 - plane, rows_of(part)], far_twin.at[rows_of(part)],
            w_send.at[part], w_recv.at[part],
            device_id=twin, device_id_type=MESH,
        )

    for k in range(2):
        f_copy(0, k).wait_recv()
    w_copy(0).start()

    @pl.when(far_first)
    def _():
        for k in range(2):
            f_copy(2, k).wait_recv()
        w_copy(2).start()
        w_copy(2).wait_recv()

    own_copy.wait_recv()
    gram(0, [whole[...]], [whole[...]], [own_twin[...]])
    scatter(0)
    for k in range(2):
        f_copy(1, k).wait_recv()
    w_copy(1).start()

    @pl.when(jnp.logical_not(far_last))
    def _():
        for k in range(3):
            next_copy(k).wait_recv()

    def join(slot, rows):
        late[slot] = rows
        begin = FAR - EARLY
        late[slot, begin:begin + SHARED, :] = (
            rows[begin:begin + SHARED].astype(F32) + next_in[slot, 0:SHARED, :].astype(F32)
        ).astype(BF16)

    for k in range(2):
        join(k, fall[k, EARLY:ROWS, :])
    for part in range(2):
        w_copy(part).wait_recv()
    join(2, far_twin[EARLY:ROWS, :])
    gram(
        1,
        [fall[plane, 0:EARLY, :], late[plane]],
        [fall[1 - plane, 0:EARLY, :], late[1 - plane]],
        [far_twin[0:EARLY, :], late[2]],
    )
    scatter(1)

    rows = lax.broadcasted_iota(jnp.int32, (NODES, NODES), 0).astype(F32)
    place = jnp.where(rows == jnp.broadcast_to(order, (NODES, NODES)), 1.0, 0.0).astype(BF16)
    full = t[0:NODES, :]
    coarse = full.astype(BF16)
    fine = (full - coarse.astype(F32)).astype(BF16)
    out_ref[...] = mm(place, coarse) + mm(place, fine)

    met(2)
    exchange(0)
    exchange(1)
    spread(0)
    spread(1)
    for part in range(2):
        g_all(part).wait_recv()

    done_faces(0)
    done_faces(1)
    own_copy.wait_send()
    w_copy(0).wait_send()
    w_copy(1).wait_send()

    @pl.when(far_first)
    def _():
        w_copy(2).wait_send()

    @pl.when(cells == 0)
    def _():
        for k in range(2):
            f_copy(2, k).wait_send()

    @pl.when(cells > 0)
    def _():
        for k in range(3):
            next_copy(k).wait_send()

    for part in range(2):
        for k in range(2):
            f_copy(part, k).wait_send()
        s_all(part).wait_send()
        z_all(part).wait_send()
        g_all(part).wait_send()


def finish(filtered, blocks, out_hbm, corr_hbm, corr, sem):
    first = pltpu.make_async_copy(filtered, out_hbm, sem.at[0])
    first.start()
    for j in range(4):
        corr[j * WIDTH:(j + 1) * WIDTH, :] = blocks[j].astype(F32).T
    second = pltpu.make_async_copy(corr, corr_hbm, sem.at[1])
    second.start()
    first.wait()
    second.wait()


def solution(mesh, sizes=(4, 4, 12)):
    ny, nx, nz = sizes
    dma = pltpu.SemaphoreType.DMA

    def body(wavefunctions, hamiltonians, connectivity, face_nodes):
        filtered, blocks = pl.pallas_call(
            lambda *refs: kernel(sizes, *refs),
            out_shape=(
                jax.ShapeDtypeStruct((NODES, WIDTH), F32),
                jax.ShapeDtypeStruct((2, 16, 16, WIDTH), BF16),
            ),
            in_specs=[pl.BlockSpec(memory_space=pltpu.HBM)] * 3,
            out_specs=(pl.BlockSpec(memory_space=pltpu.VMEM),) * 2,
            scratch_shapes=[
                pltpu.VMEM((NODES, WIDTH), BF16),
                pltpu.VMEM((NODES, NODES), BF16),
                pltpu.VMEM((1, NODES), jnp.int32),
                pltpu.VMEM((ROWS, WIDTH), BF16),
                pltpu.VMEM((ROWS, WIDTH), F32),
                pltpu.VMEM((ROWS, WIDTH), BF16),
                pltpu.VMEM((ROWS, WIDTH), BF16),
                pltpu.VMEM((ROWS, WIDTH), BF16),
                pltpu.VMEM((2, ROWS, WIDTH), BF16),
                pltpu.VMEM((ROWS, WIDTH), BF16),
                pltpu.VMEM((ROWS, WIDTH), BF16),
                pltpu.VMEM((3, 96, WIDTH), BF16),
                pltpu.VMEM((2, 2, 96, WIDTH), BF16),
                pltpu.VMEM((2, 2, 96, WIDTH), BF16),
                pltpu.VMEM((3, 96, WIDTH), BF16),
                pltpu.VMEM((2, 16, 16, WIDTH), F32),
                pltpu.VMEM((2, 16, 16, WIDTH), BF16),
                pltpu.VMEM((2, nx * ny - 1, 16, WIDTH), BF16),
                pltpu.VMEM((2, nz, 16, WIDTH), BF16),
                dma((5,)),
                dma((2, 2)), dma((2, 2)),
                pltpu.SemaphoreType.REGULAR((3,)), pltpu.SemaphoreType.REGULAR,
                dma((3,)), dma((3,)),
                dma((3, 2)), dma((3, 2)), dma((4,)), dma((4,)),
                dma((2,)), dma((2,)), dma((2,)), dma((2,)), dma((2,)), dma((2,)),
            ],
            compiler_params=pltpu.CompilerParams(
                collective_id=0, has_side_effects=True, vmem_limit_bytes=40 << 20
            ),
        )(*[pltpu.with_memory_space_constraint(a, pltpu.HBM) for a in (wavefunctions, hamiltonians, connectivity)])
        return pl.pallas_call(
            finish,
            out_shape=(
                jax.ShapeDtypeStruct((NODES, WIDTH), F32),
                jax.ShapeDtypeStruct((4 * WIDTH, WIDTH), F32),
            ),
            in_specs=[pl.BlockSpec(memory_space=pltpu.VMEM)] * 2,
            out_specs=(pl.BlockSpec(memory_space=pltpu.HBM),) * 2,
            scratch_shapes=[pltpu.VMEM((4 * WIDTH, WIDTH), F32), dma((2,))],
            compiler_params=pltpu.CompilerParams(vmem_limit_bytes=16 << 20),
        )(filtered, blocks.reshape(4, WIDTH, WIDTH))

    return jax.shard_map(
        body,
        mesh=mesh,
        in_specs=(P("cells", "bands"), P("cells", None, None), P("cells", None), P("cells", None)),
        out_specs=(P("cells", "bands"), P(None, "bands")),
        check_vma=False,
    )
```

```python
import jax
import jax.numpy as jnp
from jax import lax
from jax.experimental import pallas as pl
from jax.experimental.pallas import tpu as pltpu
from jax.sharding import PartitionSpec as P

MESH = pl.DeviceIdType.MESH
NODES = 729
SHARED = 81
FAR = NODES - SHARED
WIDTH = 128
EARLY = 640
LOW = 80
ROWS = 736
F32 = jnp.float32
BF16 = jnp.bfloat16


def mm(a, b):
    return jnp.dot(a, b, preferred_element_type=F32)


def kernel(
    sizes,
    v_hbm, h_hbm, conn_hbm,
    out_ref, res,
    v, h, conn, u, t, y1, filt, fall, own_twin, far_twin, face_out, face_in, relay,
    gram_f, gram_b, rs_in, rz,
    in_sem, face_send, face_recv, relay_sem, near, f_send, f_recv, w_send, w_recv,
    s_send, s_recv, z_send, z_recv, g_send, g_recv,
):
    ny, nx, nz = sizes
    cells = lax.axis_index("cells")
    band = lax.axis_index("bands")
    last = ny * nx * nz - 1
    z = lax.rem(cells, nz)
    x = lax.rem(cells // nz, nx)
    y = cells // (nx * nz)
    core = lax.rem(band, 2)
    plane = band // 2
    ring = 2 * ny
    half = ny // 2
    here = plane * ny + y

    def at(yy, xx, zz):
        return (yy * nx + xx) * nz + zz

    def f_peer(offset):
        there = lax.rem(here + offset + ring, ring)
        return (at(lax.rem(there, ny), x, z), (there // ny) * 2 + core)

    def x_peer(offset):
        return (at(y, lax.rem(x + offset + nx, nx), z), band)

    def z_peer(offset):
        return (at(y, x, lax.rem(z + offset + nz, nz)), band)

    def mirror(j):
        return (y, y + 1 - 2 * lax.rem(y, 2), lax.rem(y + 2, 4), 3 - y)[j]

    def xy_peer(i, j):
        return (at(mirror(j), lax.rem(x + i, nx), z), band)

    f_peers = [f_peer(half), f_peer(-half)]
    twin = (cells, band + 1 - 2 * core)
    spans = [(i, j) for i in range(nx) for j in range(ny) if i + j]
    spans.sort(key=lambda s: -(min(s[0], nx - s[0]) + s[1]))
    z_spans = sorted(range(1, nz), key=lambda k: -min(k, nz - k))

    loads = [
        pltpu.make_async_copy(conn_hbm, conn, in_sem.at[0]),
        pltpu.make_async_copy(v_hbm, v, in_sem.at[1]),
        pltpu.make_async_copy(h_hbm.at[0, pl.ds(0, 96)], h.at[pl.ds(0, 96)], in_sem.at[2]),
        pltpu.make_async_copy(
            h_hbm.at[0, pl.ds(EARLY, NODES - EARLY)], h.at[pl.ds(EARLY, NODES - EARLY)], in_sem.at[3]
        ),
        pltpu.make_async_copy(h_hbm.at[0, pl.ds(96, EARLY - 96)], h.at[pl.ds(96, EARLY - 96)], in_sem.at[4]),
    ]
    for load in loads:
        load.start()

    barrier = pltpu.get_barrier_semaphore()
    cross = (at(lax.rem(y + half, ny), x, z), (1 - plane) * 2 + 1 - core)
    peers = f_peers + [cross, twin, xy_peer(0, 1), x_peer(1), x_peer(-1), z_peer(1), z_peer(-1)]
    meetings = (
        (xy_peer(0, 1), x_peer(1), x_peer(-1), z_peer(1), z_peer(-1)),
        (x_peer(1), x_peer(-1), x_peer(2), z_peer(2), z_peer(-2)),
        (z_peer(2), z_peer(-2)),
    )

    def meet(stage):
        for peer in meetings[stage]:
            pl.semaphore_signal(near.at[stage], inc=1, device_id=peer, device_id_type=MESH)

    def met(stage):
        pl.semaphore_wait(near.at[stage], len(meetings[stage]))

    for peer in peers:
        pl.semaphore_signal(barrier, inc=1, device_id=peer, device_id_type=MESH)

    @pl.when(cells > 0)
    def _():
        pl.semaphore_signal(barrier, inc=1, device_id=(cells - 1, band), device_id_type=MESH)

    block = nx * nz
    is_after = jnp.logical_and(cells > 0, lax.rem(cells, block) == 0)
    is_before = jnp.logical_and(cells < last, lax.rem(cells, block) == block - 1)
    is_relay = jnp.logical_and(cells < last - nz, lax.rem(cells, block) == block - nz)

    @pl.when(jnp.logical_and(cells < last, jnp.logical_not(is_before)))
    def _():
        pl.semaphore_signal(barrier, inc=1, device_id=(cells + 1, band), device_id_type=MESH)

    @pl.when(is_relay)
    def _():
        pl.semaphore_signal(barrier, inc=1, device_id=(cells + nz, band), device_id_type=MESH)

    def to_relay():
        return pltpu.make_async_remote_copy(
            face_out.at[0, 0], relay, relay_sem.at[0], relay_sem.at[1],
            device_id=(cells - nz, band), device_id_type=MESH,
        )

    def from_relay():
        return pltpu.make_async_remote_copy(
            relay, face_in.at[0, 1], relay_sem.at[2], face_recv.at[0, 1],
            device_id=(cells + nz - 1, band), device_id_type=MESH,
        )

    def face_copy(step, side):
        peer = (cells - 1 + 2 * side, band)
        return pltpu.make_async_remote_copy(
            face_out.at[step, side], face_in.at[step, 1 - side],
            face_send.at[step, side], face_recv.at[step, 1 - side],
            device_id=peer, device_id_type=MESH,
        )

    def send_faces(step):
        @pl.when(cells > 0)
        def _():
            face_copy(step, 0).start()

        @pl.when(cells < last)
        def _():
            face_copy(step, 1).start()

    def wait_faces(step):
        @pl.when(cells > 0)
        def _():
            face_copy(step, 1).wait_recv()

        @pl.when(cells < last)
        def _():
            face_copy(step, 0).wait_recv()

    def done_faces(step):
        @pl.when(cells > 0)
        def _():
            face_copy(step, 0).wait_send()

        @pl.when(cells < last)
        def _():
            face_copy(step, 1).wait_send()

    @pl.when(cells == 0)
    def _():
        for step in range(2):
            face_in[step, 0] = jnp.zeros(face_in.shape[2:], BF16)

    @pl.when(cells == last)
    def _():
        for step in range(2):
            face_in[step, 1] = jnp.zeros(face_in.shape[2:], BF16)

    far_first = at(lax.rem(y + half, ny), x, z) == 0

    @pl.when(jnp.logical_not(far_first))
    def _():
        fall[0, 0:LOW, :] = jnp.zeros((LOW, WIDTH), BF16)
        fall[1, 0:LOW, :] = jnp.zeros((LOW, WIDTH), BF16)
        far_twin[0:LOW, :] = jnp.zeros((LOW, WIDTH), BF16)

    loads[0].wait()
    order = conn[...].astype(F32)
    column = jnp.broadcast_to(order, (WIDTH, NODES)).T
    lanes = lax.broadcasted_iota(jnp.int32, (NODES, WIDTH), 1).astype(F32)
    loads[1].wait()
    total = jnp.zeros((NODES, WIDTH), F32)
    for k in range(0, NODES, WIDTH):
        width = min(WIDTH, NODES - k)
        pick = jnp.where(column == lanes + float(k), 1.0, 0.0).astype(BF16)
        total += mm(pick[:, :width], v[k:k + width, :])
    u[0:NODES, :] = total.astype(BF16)

    loads[2].wait()
    loads[3].wait()
    t[0:96, :] = mm(h[0:96, :], u[0:NODES, :])
    t[EARLY:NODES, :] = mm(h[EARLY:NODES, :], u[0:NODES, :])
    face_out[0, 0, 0:SHARED, :] = t[0:SHARED, :].astype(BF16)
    face_out[0, 1, 0:SHARED, :] = t[FAR:NODES, :].astype(BF16)
    want = len(peers) + jnp.where(cells > 0, 1, 0) + jnp.where(cells < last, 1, 0)
    pl.semaphore_wait(barrier, want)
    meet(0)
    @pl.when(jnp.logical_and(cells > 0, jnp.logical_not(is_after)))
    def _():
        face_copy(0, 0).start()

    @pl.when(is_after)
    def _():
        to_relay().start()

    @pl.when(cells < last)
    def _():
        face_copy(0, 1).start()

    @pl.when(is_relay)
    def _():
        to_relay().wait_recv()
        from_relay().start()

    loads[4].wait()
    t[96:EARLY, :] = mm(h[96:EARLY, :], u[0:NODES, :])
    y1[0:NODES, :] = (0.5 * t[0:NODES, :]).astype(BF16)
    y1[0:SHARED, :] = jnp.zeros((SHARED, WIDTH), BF16)
    y1[FAR:NODES, :] = jnp.zeros((SHARED, WIDTH), BF16)
    low = t[0:SHARED, :]
    high = t[FAR:NODES, :]
    t[0:NODES, :] = mm(h[...], y1[0:NODES, :])

    wait_faces(0)
    met(0)
    meet(1)
    low1 = 0.5 * (low + face_in[0, 0, 0:SHARED, :].astype(F32))
    high1 = 0.5 * (high + face_in[0, 1, 0:SHARED, :].astype(F32))
    y1[0:WIDTH, :] = jnp.zeros((WIDTH, WIDTH), BF16)
    y1[EARLY:NODES, :] = jnp.zeros((NODES - EARLY, WIDTH), BF16)
    y1[0:SHARED, :] = low1.astype(BF16)
    y1[FAR:NODES, :] = high1.astype(BF16)

    def add_faces(lo, hi):
        t[lo:hi, :] += mm(h[lo:hi, 0:WIDTH], y1[0:WIDTH, :]) + mm(h[lo:hi, EARLY:NODES], y1[EARLY:NODES, :])

    add_faces(0, 96)
    add_faces(EARLY, NODES)
    face_out[1, 0, 0:SHARED, :] = t[0:SHARED, :].astype(BF16)
    face_out[1, 1, 0:SHARED, :] = t[FAR:NODES, :].astype(BF16)
    send_faces(1)
    add_faces(96, EARLY)

    first = jnp.where(cells == 0, jnp.float32(1.0), jnp.float32(0.0))
    t[0:NODES, :] = t[0:NODES, :] - u[0:NODES, :].astype(F32)
    filt[0:NODES, :] = t[0:NODES, :].astype(BF16)
    filt[0:SHARED, :] = (t[0:SHARED, :] * first).astype(BF16)

    def rows_of(part):
        return (pl.ds(LOW, EARLY - LOW), pl.ds(EARLY, ROWS - EARLY), pl.ds(0, LOW))[part]

    def f_copy(part, k):
        return pltpu.make_async_remote_copy(
            filt.at[rows_of(part)], fall.at[plane, rows_of(part)],
            f_send.at[part, k], f_recv.at[part, k],
            device_id=f_peers[k], device_id_type=MESH,
        )

    for k in range(2):
        f_copy(0, k).start()

    @pl.when(cells == 0)
    def _():
        for k in range(2):
            f_copy(2, k).start()

    cross_copy = pltpu.make_async_remote_copy(
        filt.at[rows_of(1)], far_twin.at[rows_of(1)],
        w_send.at[1], w_recv.at[1], device_id=cross, device_id_type=MESH,
    )

    wait_faces(1)
    t[FAR:NODES, :] += face_in[1, 1, 0:SHARED, :].astype(F32)
    filt[EARLY:NODES, :] = t[EARLY:NODES, :].astype(BF16)
    filt[NODES:ROWS, :] = jnp.zeros((ROWS - NODES, WIDTH), BF16)
    for k in range(2):
        f_copy(1, k).start()
    cross_copy.start()
    own_copy = pltpu.make_async_remote_copy(
        filt, own_twin, w_send.at[3], w_recv.at[3], device_id=twin, device_id_type=MESH
    )
    own_copy.start()
    met(1)
    meet(2)

    t[0:SHARED, :] += face_in[1, 0, 0:SHARED, :].astype(F32)
    rows = lax.broadcasted_iota(jnp.int32, (NODES, NODES), 0).astype(F32)
    place = jnp.where(rows == jnp.broadcast_to(order, (NODES, NODES)), 1.0, 0.0).astype(BF16)
    full = t[0:NODES, :]
    coarse = full.astype(BF16)
    fine = (full - coarse.astype(F32)).astype(BF16)
    out_ref[...] = mm(place, coarse) + mm(place, fine)

    def gram(part, left, one, two):
        for side, right in ((core, one), (1 - core, two)):
            block = lax.dot_general(left, right, (((0,), (0,)), ((), ())), preferred_element_type=F32)
            tiles = block.reshape(8, 16, WIDTH)
            gram_f[part, pl.ds(8 * side, 8)] = tiles
            gram_b[part, pl.ds(8 * side, 8)] = tiles.astype(BF16)

    mine = x * ny + y

    def s_copy(part, n):
        i, j = spans[n]
        shard = lax.rem(x + i, nx) * ny + mirror(j)
        return pltpu.make_async_remote_copy(
            gram_b.at[part, shard], rs_in.at[part, n],
            s_send.at[part], s_recv.at[part],
            device_id=xy_peer(i, j), device_id_type=MESH,
        )

    def z_copy(part, n):
        return pltpu.make_async_remote_copy(
            rz.at[part, z], rz.at[part, z],
            z_send.at[part], z_recv.at[part],
            device_id=z_peer(z_spans[n]), device_id_type=MESH,
        )

    def g_copy(part, n):
        i, j = spans[n]
        block = plane if part == 0 else 1 - plane
        return pltpu.make_async_remote_copy(
            res.at[block, mine], res.at[block, mine],
            g_send.at[part], g_recv.at[part],
            device_id=xy_peer(i, j), device_id_type=MESH,
        )

    def all_of(ref, send, recv):
        return pltpu.make_async_remote_copy(ref, ref, send, recv, device_id=twin, device_id_type=MESH)

    def s_all(part):
        return all_of(rs_in.at[part], s_send.at[part], s_recv.at[part])

    def z_all(part):
        return all_of(rz.at[part, pl.ds(0, nz - 1)], z_send.at[part], z_recv.at[part])

    def g_all(part):
        return all_of(rs_in.at[part], g_send.at[part], g_recv.at[part])

    def scatter(part):
        for n in range(len(spans)):
            s_copy(part, n).start()

    def exchange(part):
        total = gram_f[part, mine]
        s_all(part).wait_recv()
        for n in range(len(spans)):
            total += rs_in[part, n].astype(F32)
        rz[part, z] = total.astype(BF16)
        for n in range(len(z_spans)):
            z_copy(part, n).start()

    def spread(part):
        z_all(part).wait_recv()
        total = rz[part, 0].astype(F32)
        for k in range(1, nz):
            total += rz[part, k].astype(F32)
        res[plane if part == 0 else 1 - plane, mine] = (total / float((last + 1) * NODES)).astype(BF16)
        for n in range(len(spans)):
            g_copy(part, n).start()

    own_copy.wait_recv()
    gram(0, filt[...], filt[...], own_twin[...])
    scatter(0)

    def w_copy(part):
        return pltpu.make_async_remote_copy(
            fall.at[1 - plane, rows_of(part)], far_twin.at[rows_of(part)],
            w_send.at[part], w_recv.at[part],
            device_id=twin, device_id_type=MESH,
        )

    for k in range(2):
        f_copy(0, k).wait_recv()
    w_copy(0).start()

    @pl.when(far_first)
    def _():
        for k in range(2):
            f_copy(2, k).wait_recv()
        w_copy(2).start()
        w_copy(2).wait_recv()

    for k in range(2):
        f_copy(1, k).wait_recv()
    cross_copy.wait_recv()
    w_copy(0).wait_recv()
    gram(1, fall[plane], fall[1 - plane], far_twin[...])
    scatter(1)
    met(2)
    exchange(0)
    exchange(1)
    spread(0)
    spread(1)
    for part in range(2):
        g_all(part).wait_recv()

    @pl.when(jnp.logical_and(cells > 0, jnp.logical_not(is_after)))
    def _():
        face_copy(0, 0).wait_send()

    @pl.when(is_after)
    def _():
        to_relay().wait_send()

    @pl.when(is_relay)
    def _():
        from_relay().wait_send()

    @pl.when(cells < last)
    def _():
        face_copy(0, 1).wait_send()

    done_faces(1)
    own_copy.wait_send()
    cross_copy.wait_send()
    w_copy(0).wait_send()

    @pl.when(far_first)
    def _():
        w_copy(2).wait_send()

    @pl.when(cells == 0)
    def _():
        for k in range(2):
            f_copy(2, k).wait_send()

    for part in range(2):
        for k in range(2):
            f_copy(part, k).wait_send()
        s_all(part).wait_send()
        z_all(part).wait_send()
        g_all(part).wait_send()


def finish(filtered, blocks, out_hbm, corr_hbm, corr, sem):
    first = pltpu.make_async_copy(filtered, out_hbm, sem.at[0])
    first.start()
    for j in range(4):
        corr[j * WIDTH:(j + 1) * WIDTH, :] = blocks[j].astype(F32).T
    second = pltpu.make_async_copy(corr, corr_hbm, sem.at[1])
    second.start()
    first.wait()
    second.wait()


def solution(mesh, sizes=(4, 4, 12)):
    ny, nx, nz = sizes
    dma = pltpu.SemaphoreType.DMA

    def body(wavefunctions, hamiltonians, connectivity, face_nodes):
        filtered, blocks = pl.pallas_call(
            lambda *refs: kernel(sizes, *refs),
            out_shape=(
                jax.ShapeDtypeStruct((NODES, WIDTH), F32),
                jax.ShapeDtypeStruct((2, 16, 16, WIDTH), BF16),
            ),
            in_specs=[pl.BlockSpec(memory_space=pltpu.HBM)] * 3,
            out_specs=(pl.BlockSpec(memory_space=pltpu.VMEM),) * 2,
            scratch_shapes=[
                pltpu.VMEM((NODES, WIDTH), BF16),
                pltpu.VMEM((NODES, NODES), BF16),
                pltpu.VMEM((1, NODES), jnp.int32),
                pltpu.VMEM((ROWS, WIDTH), BF16),
                pltpu.VMEM((ROWS, WIDTH), F32),
                pltpu.VMEM((ROWS, WIDTH), BF16),
                pltpu.VMEM((ROWS, WIDTH), BF16),
                pltpu.VMEM((2, ROWS, WIDTH), BF16),
                pltpu.VMEM((ROWS, WIDTH), BF16),
                pltpu.VMEM((ROWS, WIDTH), BF16),
                pltpu.VMEM((2, 2, 96, WIDTH), BF16),
                pltpu.VMEM((2, 2, 96, WIDTH), BF16),
                pltpu.VMEM((96, WIDTH), BF16),
                pltpu.VMEM((2, 16, 16, WIDTH), F32),
                pltpu.VMEM((2, 16, 16, WIDTH), BF16),
                pltpu.VMEM((2, nx * ny - 1, 16, WIDTH), BF16),
                pltpu.VMEM((2, nz, 16, WIDTH), BF16),
                dma((5,)),
                dma((2, 2)), dma((2, 2)),
                dma((3,)),
                pltpu.SemaphoreType.REGULAR((3,)),
                dma((3, 2)), dma((3, 2)), dma((4,)), dma((4,)),
                dma((2,)), dma((2,)), dma((2,)), dma((2,)), dma((2,)), dma((2,)),
            ],
            compiler_params=pltpu.CompilerParams(
                collective_id=0, has_side_effects=True, vmem_limit_bytes=40 << 20
            ),
        )(*[pltpu.with_memory_space_constraint(a, pltpu.HBM) for a in (wavefunctions, hamiltonians, connectivity)])
        return pl.pallas_call(
            finish,
            out_shape=(
                jax.ShapeDtypeStruct((NODES, WIDTH), F32),
                jax.ShapeDtypeStruct((4 * WIDTH, WIDTH), F32),
            ),
            in_specs=[pl.BlockSpec(memory_space=pltpu.VMEM)] * 2,
            out_specs=(pl.BlockSpec(memory_space=pltpu.HBM),) * 2,
            scratch_shapes=[pltpu.VMEM((4 * WIDTH, WIDTH), F32), dma((2,))],
            compiler_params=pltpu.CompilerParams(vmem_limit_bytes=16 << 20),
        )(filtered, blocks.reshape(4, WIDTH, WIDTH))

    return jax.shard_map(
        body,
        mesh=mesh,
        in_specs=(P("cells", "bands"), P("cells", None, None), P("cells", None), P("cells", None)),
        out_specs=(P("cells", "bands"), P(None, "bands")),
        check_vma=False,
    )
```

```python
import jax
import jax.numpy as jnp
from jax import lax
from jax.experimental import pallas as pl
from jax.experimental.pallas import tpu as pltpu
from jax.sharding import PartitionSpec as P

MESH = pl.DeviceIdType.MESH
NODES = 729
SHARED = 81
FAR = NODES - SHARED
WIDTH = 128
EARLY = 640
LOW = 80
ROWS = 736
F32 = jnp.float32
BF16 = jnp.bfloat16


def mm(a, b):
    return jnp.dot(a, b, preferred_element_type=F32)


def kernel(
    sizes,
    v_hbm, h_hbm, conn_hbm,
    out_ref, res,
    v, h, conn, u, t, y1, filt, fall, own_twin, far_twin, face_out, face_in, relay,
    gram_f, gram_b, rs_in, rz,
    in_sem, face_send, face_recv, relay_sem, near, f_send, f_recv, w_send, w_recv,
    s_send, s_recv, z_send, z_recv, g_send, g_recv,
):
    ny, nx, nz = sizes
    cells = lax.axis_index("cells")
    band = lax.axis_index("bands")
    last = ny * nx * nz - 1
    z = lax.rem(cells, nz)
    x = lax.rem(cells // nz, nx)
    y = cells // (nx * nz)
    core = lax.rem(band, 2)
    plane = band // 2
    ring = 2 * ny
    half = ny // 2
    here = plane * ny + y

    def at(yy, xx, zz):
        return (yy * nx + xx) * nz + zz

    def f_peer(offset):
        there = lax.rem(here + offset + ring, ring)
        return (at(lax.rem(there, ny), x, z), (there // ny) * 2 + core)

    def x_peer(offset):
        return (at(y, lax.rem(x + offset + nx, nx), z), band)

    def z_peer(offset):
        return (at(y, x, lax.rem(z + offset + nz, nz)), band)

    def mirror(j):
        return (y, y + 1 - 2 * lax.rem(y, 2), lax.rem(y + 2, 4), 3 - y)[j]

    def xy_peer(i, j):
        return (at(mirror(j), lax.rem(x + i, nx), z), band)

    f_peers = [f_peer(half), f_peer(-half)]
    twin = (cells, band + 1 - 2 * core)
    spans = [(i, j) for i in range(nx) for j in range(ny) if i + j]
    spans.sort(key=lambda s: -(min(s[0], nx - s[0]) + s[1]))
    z_spans = sorted(range(1, nz), key=lambda k: -min(k, nz - k))

    loads = [
        pltpu.make_async_copy(conn_hbm, conn, in_sem.at[0]),
        pltpu.make_async_copy(v_hbm, v, in_sem.at[1]),
        pltpu.make_async_copy(h_hbm.at[0, pl.ds(0, 96)], h.at[pl.ds(0, 96)], in_sem.at[2]),
        pltpu.make_async_copy(
            h_hbm.at[0, pl.ds(EARLY, NODES - EARLY)], h.at[pl.ds(EARLY, NODES - EARLY)], in_sem.at[3]
        ),
        pltpu.make_async_copy(h_hbm.at[0, pl.ds(96, EARLY - 96)], h.at[pl.ds(96, EARLY - 96)], in_sem.at[4]),
    ]
    for load in loads:
        load.start()

    barrier = pltpu.get_barrier_semaphore()
    cross = (at(lax.rem(y + half, ny), x, z), (1 - plane) * 2 + 1 - core)
    peers = f_peers + [cross, twin, xy_peer(0, 1), x_peer(1), x_peer(-1), z_peer(1), z_peer(-1)]
    meetings = (
        (xy_peer(0, 1), x_peer(1), x_peer(-1), z_peer(1), z_peer(-1)),
        (x_peer(1), x_peer(-1), x_peer(2), z_peer(2), z_peer(-2)),
        (z_peer(2), z_peer(-2)),
    )

    def meet(stage):
        for peer in meetings[stage]:
            pl.semaphore_signal(near.at[stage], inc=1, device_id=peer, device_id_type=MESH)

    def met(stage):
        pl.semaphore_wait(near.at[stage], len(meetings[stage]))

    for peer in peers:
        pl.semaphore_signal(barrier, inc=1, device_id=peer, device_id_type=MESH)

    @pl.when(cells > 0)
    def _():
        pl.semaphore_signal(barrier, inc=1, device_id=(cells - 1, band), device_id_type=MESH)

    block = nx * nz
    is_after = jnp.logical_and(cells > 0, lax.rem(cells, block) == 0)
    is_before = jnp.logical_and(cells < last, lax.rem(cells, block) == block - 1)
    is_relay = jnp.logical_and(cells < last - nz, lax.rem(cells, block) == block - nz)

    @pl.when(jnp.logical_and(cells < last, jnp.logical_not(is_before)))
    def _():
        pl.semaphore_signal(barrier, inc=1, device_id=(cells + 1, band), device_id_type=MESH)

    @pl.when(is_relay)
    def _():
        pl.semaphore_signal(barrier, inc=1, device_id=(cells + nz, band), device_id_type=MESH)

    def to_relay():
        return pltpu.make_async_remote_copy(
            face_out.at[0, 0], relay, relay_sem.at[0], relay_sem.at[1],
            device_id=(cells - nz, band), device_id_type=MESH,
        )

    def from_relay():
        return pltpu.make_async_remote_copy(
            relay, face_in.at[0, 1], relay_sem.at[2], face_recv.at[0, 1],
            device_id=(cells + nz - 1, band), device_id_type=MESH,
        )

    def face_copy(step, side):
        peer = (cells - 1 + 2 * side, band)
        return pltpu.make_async_remote_copy(
            face_out.at[step, side], face_in.at[step, 1 - side],
            face_send.at[step, side], face_recv.at[step, 1 - side],
            device_id=peer, device_id_type=MESH,
        )

    def send_faces(step):
        @pl.when(cells > 0)
        def _():
            face_copy(step, 0).start()

        @pl.when(cells < last)
        def _():
            face_copy(step, 1).start()

    def wait_faces(step):
        @pl.when(cells > 0)
        def _():
            face_copy(step, 1).wait_recv()

        @pl.when(cells < last)
        def _():
            face_copy(step, 0).wait_recv()

    def done_faces(step):
        @pl.when(cells > 0)
        def _():
            face_copy(step, 0).wait_send()

        @pl.when(cells < last)
        def _():
            face_copy(step, 1).wait_send()

    @pl.when(cells == 0)
    def _():
        for step in range(2):
            face_in[step, 0] = jnp.zeros(face_in.shape[2:], BF16)

    @pl.when(cells == last)
    def _():
        for step in range(2):
            face_in[step, 1] = jnp.zeros(face_in.shape[2:], BF16)

    far_first = at(lax.rem(y + half, ny), x, z) == 0

    @pl.when(jnp.logical_not(far_first))
    def _():
        fall[0, 0:LOW, :] = jnp.zeros((LOW, WIDTH), BF16)
        fall[1, 0:LOW, :] = jnp.zeros((LOW, WIDTH), BF16)
        far_twin[0:LOW, :] = jnp.zeros((LOW, WIDTH), BF16)

    loads[0].wait()
    order = conn[...].astype(F32)
    column = jnp.broadcast_to(order, (WIDTH, NODES)).T
    lanes = lax.broadcasted_iota(jnp.int32, (NODES, WIDTH), 1).astype(F32)
    loads[1].wait()
    total = jnp.zeros((NODES, WIDTH), F32)
    for k in range(0, NODES, WIDTH):
        width = min(WIDTH, NODES - k)
        pick = jnp.where(column == lanes + float(k), 1.0, 0.0).astype(BF16)
        total += mm(pick[:, :width], v[k:k + width, :])
    u[0:NODES, :] = total.astype(BF16)

    loads[2].wait()
    loads[3].wait()
    t[0:96, :] = mm(h[0:96, :], u[0:NODES, :])
    t[EARLY:NODES, :] = mm(h[EARLY:NODES, :], u[0:NODES, :])
    face_out[0, 0, 0:SHARED, :] = t[0:SHARED, :].astype(BF16)
    face_out[0, 1, 0:SHARED, :] = t[FAR:NODES, :].astype(BF16)
    want = len(peers) + jnp.where(cells > 0, 1, 0) + jnp.where(cells < last, 1, 0)
    pl.semaphore_wait(barrier, want)
    meet(0)
    @pl.when(jnp.logical_and(cells > 0, jnp.logical_not(is_after)))
    def _():
        face_copy(0, 0).start()

    @pl.when(is_after)
    def _():
        to_relay().start()

    @pl.when(cells < last)
    def _():
        face_copy(0, 1).start()

    @pl.when(is_relay)
    def _():
        to_relay().wait_recv()
        from_relay().start()

    loads[4].wait()
    t[96:EARLY, :] = mm(h[96:EARLY, :], u[0:NODES, :])
    y1[0:NODES, :] = (0.5 * t[0:NODES, :]).astype(BF16)
    y1[0:SHARED, :] = jnp.zeros((SHARED, WIDTH), BF16)
    y1[FAR:NODES, :] = jnp.zeros((SHARED, WIDTH), BF16)
    low = t[0:SHARED, :]
    high = t[FAR:NODES, :]
    t[0:NODES, :] = mm(h[...], y1[0:NODES, :])

    wait_faces(0)
    met(0)
    meet(1)
    low1 = 0.5 * (low + face_in[0, 0, 0:SHARED, :].astype(F32))
    high1 = 0.5 * (high + face_in[0, 1, 0:SHARED, :].astype(F32))
    y1[0:WIDTH, :] = jnp.zeros((WIDTH, WIDTH), BF16)
    y1[EARLY:NODES, :] = jnp.zeros((NODES - EARLY, WIDTH), BF16)
    y1[0:SHARED, :] = low1.astype(BF16)
    y1[FAR:NODES, :] = high1.astype(BF16)

    def add_faces(lo, hi):
        t[lo:hi, :] += mm(h[lo:hi, 0:WIDTH], y1[0:WIDTH, :]) + mm(h[lo:hi, EARLY:NODES], y1[EARLY:NODES, :])

    add_faces(0, 96)
    add_faces(EARLY, NODES)
    face_out[1, 0, 0:SHARED, :] = t[0:SHARED, :].astype(BF16)
    face_out[1, 1, 0:SHARED, :] = t[FAR:NODES, :].astype(BF16)
    send_faces(1)
    add_faces(96, EARLY)

    first = jnp.where(cells == 0, jnp.float32(1.0), jnp.float32(0.0))
    t[0:NODES, :] = t[0:NODES, :] - u[0:NODES, :].astype(F32)
    filt[0:NODES, :] = t[0:NODES, :].astype(BF16)
    filt[0:SHARED, :] = (t[0:SHARED, :] * first).astype(BF16)

    def rows_of(part):
        return (pl.ds(LOW, EARLY - LOW), pl.ds(EARLY, ROWS - EARLY), pl.ds(0, LOW))[part]

    def f_copy(part, k):
        return pltpu.make_async_remote_copy(
            filt.at[rows_of(part)], fall.at[plane, rows_of(part)],
            f_send.at[part, k], f_recv.at[part, plane],
            device_id=f_peers[k], device_id_type=MESH,
        )

    def f_wait(part, source):
        pltpu.make_async_remote_copy(
            filt.at[rows_of(part)], fall.at[source, rows_of(part)],
            f_send.at[part, 0], f_recv.at[part, source],
            device_id=f_peers[0], device_id_type=MESH,
        ).wait_recv()

    for k in range(2):
        f_copy(0, k).start()

    @pl.when(cells == 0)
    def _():
        for k in range(2):
            f_copy(2, k).start()

    cross_copy = pltpu.make_async_remote_copy(
        filt.at[rows_of(1)], far_twin.at[rows_of(1)],
        w_send.at[1], w_recv.at[1], device_id=cross, device_id_type=MESH,
    )

    wait_faces(1)
    t[FAR:NODES, :] += face_in[1, 1, 0:SHARED, :].astype(F32)
    filt[EARLY:NODES, :] = t[EARLY:NODES, :].astype(BF16)
    filt[NODES:ROWS, :] = jnp.zeros((ROWS - NODES, WIDTH), BF16)
    for k in range(2):
        f_copy(1, k).start()
    cross_copy.start()
    own_copy = pltpu.make_async_remote_copy(
        filt, own_twin, w_send.at[3], w_recv.at[3], device_id=twin, device_id_type=MESH
    )
    own_copy.start()
    met(1)
    meet(2)


    def gram(part, left, one, two):
        for side, right in ((core, one), (1 - core, two)):
            block = lax.dot_general(left, right, (((0,), (0,)), ((), ())), preferred_element_type=F32)
            tiles = block.reshape(8, 16, WIDTH)
            gram_f[part, pl.ds(8 * side, 8)] = tiles
            gram_b[part, pl.ds(8 * side, 8)] = tiles.astype(BF16)

    mine = x * ny + y

    def s_copy(part, n):
        i, j = spans[n]
        shard = lax.rem(x + i, nx) * ny + mirror(j)
        return pltpu.make_async_remote_copy(
            gram_b.at[part, shard], rs_in.at[part, n],
            s_send.at[part], s_recv.at[part],
            device_id=xy_peer(i, j), device_id_type=MESH,
        )

    def z_copy(part, n):
        return pltpu.make_async_remote_copy(
            rz.at[part, z], rz.at[part, z],
            z_send.at[part], z_recv.at[part],
            device_id=z_peer(z_spans[n]), device_id_type=MESH,
        )

    def g_copy(part, n):
        i, j = spans[n]
        block = plane if part == 0 else 1 - plane
        return pltpu.make_async_remote_copy(
            res.at[block, mine], res.at[block, mine],
            g_send.at[part], g_recv.at[part],
            device_id=xy_peer(i, j), device_id_type=MESH,
        )

    def all_of(ref, send, recv):
        return pltpu.make_async_remote_copy(ref, ref, send, recv, device_id=twin, device_id_type=MESH)

    def s_all(part):
        return all_of(rs_in.at[part], s_send.at[part], s_recv.at[part])

    def z_all(part):
        return all_of(rz.at[part, pl.ds(0, nz - 1)], z_send.at[part], z_recv.at[part])

    def g_all(part):
        return all_of(rs_in.at[part], g_send.at[part], g_recv.at[part])

    def scatter(part):
        for n in range(len(spans)):
            s_copy(part, n).start()

    def exchange(part):
        total = gram_f[part, mine]
        s_all(part).wait_recv()
        for n in range(len(spans)):
            total += rs_in[part, n].astype(F32)
        rz[part, z] = total.astype(BF16)
        for n in range(len(z_spans)):
            z_copy(part, n).start()

    def spread(part):
        z_all(part).wait_recv()
        total = rz[part, 0].astype(F32)
        for k in range(1, nz):
            total += rz[part, k].astype(F32)
        res[plane if part == 0 else 1 - plane, mine] = (total / float((last + 1) * NODES)).astype(BF16)
        for n in range(len(spans)):
            g_copy(part, n).start()

    own_copy.wait_recv()
    gram(0, filt[...], filt[...], own_twin[...])
    scatter(0)

    def w_copy(part):
        return pltpu.make_async_remote_copy(
            fall.at[1 - plane, rows_of(part)], far_twin.at[rows_of(part)],
            w_send.at[part], w_recv.at[part],
            device_id=twin, device_id_type=MESH,
        )

    f_wait(0, 1 - plane)
    w_copy(0).start()
    f_wait(0, plane)

    @pl.when(far_first)
    def _():
        for k in range(2):
            f_wait(2, k)
        w_copy(2).start()
        w_copy(2).wait_recv()

    for k in range(2):
        f_wait(1, k)
    cross_copy.wait_recv()
    w_copy(0).wait_recv()
    gram(1, fall[plane], fall[1 - plane], far_twin[...])
    scatter(1)
    t[0:SHARED, :] += face_in[1, 0, 0:SHARED, :].astype(F32)
    rows = lax.broadcasted_iota(jnp.int32, (NODES, NODES), 0).astype(F32)
    place = jnp.where(rows == jnp.broadcast_to(order, (NODES, NODES)), 1.0, 0.0).astype(BF16)
    full = t[0:NODES, :]
    coarse = full.astype(BF16)
    fine = (full - coarse.astype(F32)).astype(BF16)
    out_ref[...] = mm(place, coarse) + mm(place, fine)
    met(2)
    exchange(0)
    exchange(1)
    spread(0)
    spread(1)
    for part in range(2):
        g_all(part).wait_recv()

    @pl.when(jnp.logical_and(cells > 0, jnp.logical_not(is_after)))
    def _():
        face_copy(0, 0).wait_send()

    @pl.when(is_after)
    def _():
        to_relay().wait_send()

    @pl.when(is_relay)
    def _():
        from_relay().wait_send()

    @pl.when(cells < last)
    def _():
        face_copy(0, 1).wait_send()

    done_faces(1)
    own_copy.wait_send()
    cross_copy.wait_send()
    w_copy(0).wait_send()

    @pl.when(far_first)
    def _():
        w_copy(2).wait_send()

    @pl.when(cells == 0)
    def _():
        for k in range(2):
            f_copy(2, k).wait_send()

    for part in range(2):
        for k in range(2):
            f_copy(part, k).wait_send()
        s_all(part).wait_send()
        z_all(part).wait_send()
        g_all(part).wait_send()


def finish(filtered, blocks, out_hbm, corr_hbm, corr, sem):
    first = pltpu.make_async_copy(filtered, out_hbm, sem.at[0])
    first.start()
    for j in range(4):
        corr[j * WIDTH:(j + 1) * WIDTH, :] = blocks[j].astype(F32).T
    second = pltpu.make_async_copy(corr, corr_hbm, sem.at[1])
    second.start()
    first.wait()
    second.wait()


def solution(mesh, sizes=(4, 4, 12)):
    ny, nx, nz = sizes
    dma = pltpu.SemaphoreType.DMA

    def body(wavefunctions, hamiltonians, connectivity, face_nodes):
        filtered, blocks = pl.pallas_call(
            lambda *refs: kernel(sizes, *refs),
            out_shape=(
                jax.ShapeDtypeStruct((NODES, WIDTH), F32),
                jax.ShapeDtypeStruct((2, 16, 16, WIDTH), BF16),
            ),
            in_specs=[pl.BlockSpec(memory_space=pltpu.HBM)] * 3,
            out_specs=(pl.BlockSpec(memory_space=pltpu.VMEM),) * 2,
            scratch_shapes=[
                pltpu.VMEM((NODES, WIDTH), BF16),
                pltpu.VMEM((NODES, NODES), BF16),
                pltpu.VMEM((1, NODES), jnp.int32),
                pltpu.VMEM((ROWS, WIDTH), BF16),
                pltpu.VMEM((ROWS, WIDTH), F32),
                pltpu.VMEM((ROWS, WIDTH), BF16),
                pltpu.VMEM((ROWS, WIDTH), BF16),
                pltpu.VMEM((2, ROWS, WIDTH), BF16),
                pltpu.VMEM((ROWS, WIDTH), BF16),
                pltpu.VMEM((ROWS, WIDTH), BF16),
                pltpu.VMEM((2, 2, 96, WIDTH), BF16),
                pltpu.VMEM((2, 2, 96, WIDTH), BF16),
                pltpu.VMEM((96, WIDTH), BF16),
                pltpu.VMEM((2, 16, 16, WIDTH), F32),
                pltpu.VMEM((2, 16, 16, WIDTH), BF16),
                pltpu.VMEM((2, nx * ny - 1, 16, WIDTH), BF16),
                pltpu.VMEM((2, nz, 16, WIDTH), BF16),
                dma((5,)),
                dma((2, 2)), dma((2, 2)),
                dma((3,)),
                pltpu.SemaphoreType.REGULAR((3,)),
                dma((3, 2)), dma((3, 2)), dma((4,)), dma((4,)),
                dma((2,)), dma((2,)), dma((2,)), dma((2,)), dma((2,)), dma((2,)),
            ],
            compiler_params=pltpu.CompilerParams(
                collective_id=0, has_side_effects=True, vmem_limit_bytes=40 << 20
            ),
        )(*[pltpu.with_memory_space_constraint(a, pltpu.HBM) for a in (wavefunctions, hamiltonians, connectivity)])
        return pl.pallas_call(
            finish,
            out_shape=(
                jax.ShapeDtypeStruct((NODES, WIDTH), F32),
                jax.ShapeDtypeStruct((4 * WIDTH, WIDTH), F32),
            ),
            in_specs=[pl.BlockSpec(memory_space=pltpu.VMEM)] * 2,
            out_specs=(pl.BlockSpec(memory_space=pltpu.HBM),) * 2,
            scratch_shapes=[pltpu.VMEM((4 * WIDTH, WIDTH), F32), dma((2,))],
            compiler_params=pltpu.CompilerParams(vmem_limit_bytes=16 << 20),
        )(filtered, blocks.reshape(4, WIDTH, WIDTH))

    return jax.shard_map(
        body,
        mesh=mesh,
        in_specs=(P("cells", "bands"), P("cells", None, None), P("cells", None), P("cells", None)),
        out_specs=(P("cells", "bands"), P(None, "bands")),
        check_vma=False,
    )
```

```python
import jax
import jax.numpy as jnp
from jax import lax
from jax.experimental import pallas as pl
from jax.experimental.pallas import tpu as pltpu
from jax.sharding import PartitionSpec as P

MESH = pl.DeviceIdType.MESH
NODES = 729
SHARED = 81
FAR = NODES - SHARED
WIDTH = 128
EARLY = 640
LOW = 80
ROWS = 736
F32 = jnp.float32
BF16 = jnp.bfloat16


def mm(a, b):
    return jnp.dot(a, b, preferred_element_type=F32)


def kernel(
    sizes,
    v_hbm, h_hbm, conn_hbm,
    out_ref, res,
    v, h, conn, u, t, y1, filt, fall, own_twin, far_twin, face_out, face_in, relay,
    gram_f, gram_b, rs_in, rz,
    in_sem, face_send, face_recv, relay_sem, near, f_send, f_recv, w_send, w_recv,
    s_send, s_recv, z_send, z_recv, g_send, g_recv,
):
    ny, nx, nz = sizes
    cells = lax.axis_index("cells")
    band = lax.axis_index("bands")
    last = ny * nx * nz - 1
    z = lax.rem(cells, nz)
    x = lax.rem(cells // nz, nx)
    y = cells // (nx * nz)
    core = lax.rem(band, 2)
    plane = band // 2
    ring = 2 * ny
    half = ny // 2
    here = plane * ny + y

    def at(yy, xx, zz):
        return (yy * nx + xx) * nz + zz

    def f_peer(offset):
        there = lax.rem(here + offset + ring, ring)
        return (at(lax.rem(there, ny), x, z), (there // ny) * 2 + core)

    def x_peer(offset):
        return (at(y, lax.rem(x + offset + nx, nx), z), band)

    def z_peer(offset):
        return (at(y, x, lax.rem(z + offset + nz, nz)), band)

    def mirror(j):
        return (y, y + 1 - 2 * lax.rem(y, 2), lax.rem(y + 2, 4), 3 - y)[j]

    def xy_peer(i, j):
        return (at(mirror(j), lax.rem(x + i, nx), z), band)

    f_peers = [f_peer(half), f_peer(-half)]
    twin = (cells, band + 1 - 2 * core)
    spans = [(i, j) for i in range(nx) for j in range(ny) if i + j]
    spans.sort(key=lambda s: -(min(s[0], nx - s[0]) + s[1]))
    z_spans = sorted(range(1, nz), key=lambda k: -min(k, nz - k))

    loads = [
        pltpu.make_async_copy(conn_hbm, conn, in_sem.at[0]),
        pltpu.make_async_copy(v_hbm, v, in_sem.at[1]),
        pltpu.make_async_copy(h_hbm.at[0, pl.ds(0, 96)], h.at[pl.ds(0, 96)], in_sem.at[2]),
        pltpu.make_async_copy(
            h_hbm.at[0, pl.ds(EARLY, NODES - EARLY)], h.at[pl.ds(EARLY, NODES - EARLY)], in_sem.at[3]
        ),
        pltpu.make_async_copy(h_hbm.at[0, pl.ds(96, EARLY - 96)], h.at[pl.ds(96, EARLY - 96)], in_sem.at[4]),
    ]
    barrier = pltpu.get_barrier_semaphore()
    cross = (at(lax.rem(y + half, ny), x, z), (1 - plane) * 2 + 1 - core)
    peers = f_peers + [cross, twin, xy_peer(0, 1), x_peer(1), x_peer(-1), z_peer(1), z_peer(-1)]
    meetings = (
        (xy_peer(0, 1), x_peer(1), x_peer(-1), z_peer(1), z_peer(-1)),
        (x_peer(1), x_peer(-1), x_peer(2), z_peer(2), z_peer(-2)),
        (z_peer(2), z_peer(-2)),
    )

    def meet(stage):
        for peer in meetings[stage]:
            pl.semaphore_signal(near.at[stage], inc=1, device_id=peer, device_id_type=MESH)

    def met(stage):
        pl.semaphore_wait(near.at[stage], len(meetings[stage]))

    for peer in peers:
        pl.semaphore_signal(barrier, inc=1, device_id=peer, device_id_type=MESH)

    @pl.when(cells > 0)
    def _():
        pl.semaphore_signal(barrier, inc=1, device_id=(cells - 1, band), device_id_type=MESH)

    block = nx * nz
    is_after = jnp.logical_and(cells > 0, lax.rem(cells, block) == 0)
    is_before = jnp.logical_and(cells < last, lax.rem(cells, block) == block - 1)
    is_relay = jnp.logical_and(cells < last - nz, lax.rem(cells, block) == block - nz)

    @pl.when(jnp.logical_and(cells < last, jnp.logical_not(is_before)))
    def _():
        pl.semaphore_signal(barrier, inc=1, device_id=(cells + 1, band), device_id_type=MESH)

    @pl.when(is_relay)
    def _():
        pl.semaphore_signal(barrier, inc=1, device_id=(cells + nz, band), device_id_type=MESH)

    def to_relay():
        return pltpu.make_async_remote_copy(
            face_out.at[0, 0], relay, relay_sem.at[0], relay_sem.at[1],
            device_id=(cells - nz, band), device_id_type=MESH,
        )

    def from_relay():
        return pltpu.make_async_remote_copy(
            relay, face_in.at[0, 1], relay_sem.at[2], face_recv.at[0, 1],
            device_id=(cells + nz - 1, band), device_id_type=MESH,
        )

    for load in loads:
        load.start()

    def face_copy(step, side):
        peer = (cells - 1 + 2 * side, band)
        return pltpu.make_async_remote_copy(
            face_out.at[step, side], face_in.at[step, 1 - side],
            face_send.at[step, side], face_recv.at[step, 1 - side],
            device_id=peer, device_id_type=MESH,
        )

    def send_faces(step):
        @pl.when(cells > 0)
        def _():
            face_copy(step, 0).start()

        @pl.when(cells < last)
        def _():
            face_copy(step, 1).start()

    def wait_faces(step):
        @pl.when(cells > 0)
        def _():
            face_copy(step, 1).wait_recv()

        @pl.when(cells < last)
        def _():
            face_copy(step, 0).wait_recv()

    def done_faces(step):
        @pl.when(cells > 0)
        def _():
            face_copy(step, 0).wait_send()

        @pl.when(cells < last)
        def _():
            face_copy(step, 1).wait_send()

    @pl.when(cells == 0)
    def _():
        for step in range(2):
            face_in[step, 0] = jnp.zeros(face_in.shape[2:], BF16)

    @pl.when(cells == last)
    def _():
        for step in range(2):
            face_in[step, 1] = jnp.zeros(face_in.shape[2:], BF16)

    far_first = at(lax.rem(y + half, ny), x, z) == 0

    @pl.when(jnp.logical_not(far_first))
    def _():
        fall[0, 0:LOW, :] = jnp.zeros((LOW, WIDTH), BF16)
        fall[1, 0:LOW, :] = jnp.zeros((LOW, WIDTH), BF16)
        far_twin[0:LOW, :] = jnp.zeros((LOW, WIDTH), BF16)

    loads[0].wait()
    order = conn[...].astype(F32)
    column = jnp.broadcast_to(order, (WIDTH, NODES)).T
    lanes = lax.broadcasted_iota(jnp.int32, (NODES, WIDTH), 1).astype(F32)
    loads[1].wait()
    total = jnp.zeros((NODES, WIDTH), F32)
    for k in range(0, NODES, WIDTH):
        width = min(WIDTH, NODES - k)
        pick = jnp.where(column == lanes + float(k), 1.0, 0.0).astype(BF16)
        total += mm(pick[:, :width], v[k:k + width, :])
    u[0:NODES, :] = total.astype(BF16)

    loads[2].wait()
    loads[3].wait()
    t[0:96, :] = mm(h[0:96, :], u[0:NODES, :])
    t[EARLY:NODES, :] = mm(h[EARLY:NODES, :], u[0:NODES, :])
    face_out[0, 0, 0:SHARED, :] = t[0:SHARED, :].astype(BF16)
    face_out[0, 1, 0:SHARED, :] = t[FAR:NODES, :].astype(BF16)
    want = len(peers) + jnp.where(cells > 0, 1, 0) + jnp.where(cells < last, 1, 0)
    pl.semaphore_wait(barrier, want)
    @pl.when(jnp.logical_and(cells > 0, jnp.logical_not(is_after)))
    def _():
        face_copy(0, 0).start()

    @pl.when(is_after)
    def _():
        to_relay().start()

    @pl.when(cells < last)
    def _():
        face_copy(0, 1).start()

    meet(0)

    @pl.when(is_relay)
    def _():
        to_relay().wait_recv()
        from_relay().start()

    loads[4].wait()
    t[96:EARLY, :] = mm(h[96:EARLY, :], u[0:NODES, :])
    y1[0:NODES, :] = (0.5 * t[0:NODES, :]).astype(BF16)
    y1[0:SHARED, :] = jnp.zeros((SHARED, WIDTH), BF16)
    y1[FAR:NODES, :] = jnp.zeros((SHARED, WIDTH), BF16)
    low = t[0:SHARED, :]
    high = t[FAR:NODES, :]
    t[0:NODES, :] = mm(h[...], y1[0:NODES, :])

    wait_faces(0)
    met(0)
    meet(1)
    low1 = 0.5 * (low + face_in[0, 0, 0:SHARED, :].astype(F32))
    high1 = 0.5 * (high + face_in[0, 1, 0:SHARED, :].astype(F32))
    y1[0:WIDTH, :] = jnp.zeros((WIDTH, WIDTH), BF16)
    y1[EARLY:NODES, :] = jnp.zeros((NODES - EARLY, WIDTH), BF16)
    y1[0:SHARED, :] = low1.astype(BF16)
    y1[FAR:NODES, :] = high1.astype(BF16)

    def add_faces(lo, hi):
        t[lo:hi, :] += mm(h[lo:hi, 0:WIDTH], y1[0:WIDTH, :]) + mm(h[lo:hi, EARLY:NODES], y1[EARLY:NODES, :])

    add_faces(0, 96)
    add_faces(EARLY, NODES)
    face_out[1, 0, 0:SHARED, :] = t[0:SHARED, :].astype(BF16)
    face_out[1, 1, 0:SHARED, :] = t[FAR:NODES, :].astype(BF16)
    send_faces(1)
    add_faces(96, EARLY)

    first = jnp.where(cells == 0, jnp.float32(1.0), jnp.float32(0.0))
    t[0:NODES, :] = t[0:NODES, :] - u[0:NODES, :].astype(F32)
    filt[0:NODES, :] = t[0:NODES, :].astype(BF16)
    filt[0:SHARED, :] = (t[0:SHARED, :] * first).astype(BF16)

    def rows_of(part):
        return (pl.ds(LOW, EARLY - LOW), pl.ds(EARLY, ROWS - EARLY), pl.ds(0, LOW))[part]

    def f_copy(part, k):
        return pltpu.make_async_remote_copy(
            filt.at[rows_of(part)], fall.at[plane, rows_of(part)],
            f_send.at[part, k], f_recv.at[part, plane],
            device_id=f_peers[k], device_id_type=MESH,
        )

    def f_wait(part, source):
        pltpu.make_async_remote_copy(
            filt.at[rows_of(part)], fall.at[source, rows_of(part)],
            f_send.at[part, 0], f_recv.at[part, source],
            device_id=f_peers[0], device_id_type=MESH,
        ).wait_recv()

    for k in range(2):
        f_copy(0, k).start()

    @pl.when(cells == 0)
    def _():
        for k in range(2):
            f_copy(2, k).start()

    cross_copy = pltpu.make_async_remote_copy(
        filt.at[rows_of(1)], far_twin.at[rows_of(1)],
        w_send.at[1], w_recv.at[1], device_id=cross, device_id_type=MESH,
    )

    wait_faces(1)
    t[FAR:NODES, :] += face_in[1, 1, 0:SHARED, :].astype(F32)
    filt[EARLY:NODES, :] = t[EARLY:NODES, :].astype(BF16)
    filt[NODES:ROWS, :] = jnp.zeros((ROWS - NODES, WIDTH), BF16)
    for k in range(2):
        f_copy(1, k).start()
    cross_copy.start()
    own_copy = pltpu.make_async_remote_copy(
        filt, own_twin, w_send.at[3], w_recv.at[3], device_id=twin, device_id_type=MESH
    )
    own_copy.start()
    met(1)
    meet(2)


    def gram(part, left, one, two):
        for side, right in ((core, one), (1 - core, two)):
            block = lax.dot_general(left, right, (((0,), (0,)), ((), ())), preferred_element_type=F32)
            tiles = block.reshape(8, 16, WIDTH)
            gram_f[part, pl.ds(8 * side, 8)] = tiles
            gram_b[part, pl.ds(8 * side, 8)] = tiles.astype(BF16)

    mine = x * ny + y

    def s_copy(part, n):
        i, j = spans[n]
        shard = lax.rem(x + i, nx) * ny + mirror(j)
        return pltpu.make_async_remote_copy(
            gram_b.at[part, shard], rs_in.at[part, n],
            s_send.at[part], s_recv.at[part],
            device_id=xy_peer(i, j), device_id_type=MESH,
        )

    def z_copy(part, n):
        return pltpu.make_async_remote_copy(
            rz.at[part, z], rz.at[part, z],
            z_send.at[part], z_recv.at[part],
            device_id=z_peer(z_spans[n]), device_id_type=MESH,
        )

    def g_copy(part, n):
        i, j = spans[n]
        block = plane if part == 0 else 1 - plane
        return pltpu.make_async_remote_copy(
            res.at[block, mine], res.at[block, mine],
            g_send.at[part], g_recv.at[part],
            device_id=xy_peer(i, j), device_id_type=MESH,
        )

    def all_of(ref, send, recv):
        return pltpu.make_async_remote_copy(ref, ref, send, recv, device_id=twin, device_id_type=MESH)

    def s_all(part):
        return all_of(rs_in.at[part], s_send.at[part], s_recv.at[part])

    def z_all(part):
        return all_of(rz.at[part, pl.ds(0, nz - 1)], z_send.at[part], z_recv.at[part])

    def g_all(part):
        return all_of(rs_in.at[part], g_send.at[part], g_recv.at[part])

    def scatter(part):
        for n in range(len(spans)):
            s_copy(part, n).start()

    def exchange(part):
        total = gram_f[part, mine]
        s_all(part).wait_recv()
        for n in range(len(spans)):
            total += rs_in[part, n].astype(F32)
        rz[part, z] = total.astype(BF16)
        for n in range(len(z_spans)):
            z_copy(part, n).start()

    def spread(part):
        z_all(part).wait_recv()
        total = rz[part, 0].astype(F32)
        for k in range(1, nz):
            total += rz[part, k].astype(F32)
        res[plane if part == 0 else 1 - plane, mine] = (total / float((last + 1) * NODES)).astype(BF16)
        for n in range(len(spans)):
            g_copy(part, n).start()

    own_copy.wait_recv()
    gram(0, filt[...], filt[...], own_twin[...])
    scatter(0)

    def w_copy(part):
        return pltpu.make_async_remote_copy(
            fall.at[1 - plane, rows_of(part)], far_twin.at[rows_of(part)],
            w_send.at[part], w_recv.at[part],
            device_id=twin, device_id_type=MESH,
        )

    f_wait(0, 1 - plane)
    w_copy(0).start()
    f_wait(0, plane)

    @pl.when(far_first)
    def _():
        for k in range(2):
            f_wait(2, k)
        w_copy(2).start()
        w_copy(2).wait_recv()

    for k in range(2):
        f_wait(1, k)
    cross_copy.wait_recv()
    w_copy(0).wait_recv()
    gram(1, fall[plane], fall[1 - plane], far_twin[...])
    scatter(1)
    t[0:SHARED, :] += face_in[1, 0, 0:SHARED, :].astype(F32)
    rows = lax.broadcasted_iota(jnp.int32, (NODES, NODES), 0).astype(F32)
    place = jnp.where(rows == jnp.broadcast_to(order, (NODES, NODES)), 1.0, 0.0).astype(BF16)
    full = t[0:NODES, :]
    coarse = full.astype(BF16)
    fine = (full - coarse.astype(F32)).astype(BF16)
    out_ref[...] = mm(place, coarse) + mm(place, fine)
    met(2)
    exchange(0)
    exchange(1)
    spread(0)
    spread(1)
    for part in range(2):
        g_all(part).wait_recv()

    @pl.when(jnp.logical_and(cells > 0, jnp.logical_not(is_after)))
    def _():
        face_copy(0, 0).wait_send()

    @pl.when(is_after)
    def _():
        to_relay().wait_send()

    @pl.when(is_relay)
    def _():
        from_relay().wait_send()

    @pl.when(cells < last)
    def _():
        face_copy(0, 1).wait_send()

    done_faces(1)
    own_copy.wait_send()
    cross_copy.wait_send()
    w_copy(0).wait_send()

    @pl.when(far_first)
    def _():
        w_copy(2).wait_send()

    @pl.when(cells == 0)
    def _():
        for k in range(2):
            f_copy(2, k).wait_send()

    for part in range(2):
        for k in range(2):
            f_copy(part, k).wait_send()
        s_all(part).wait_send()
        z_all(part).wait_send()
        g_all(part).wait_send()


def finish(filtered, blocks, out_hbm, corr_hbm, corr, sem):
    first = pltpu.make_async_copy(filtered, out_hbm, sem.at[0])
    first.start()
    for j in range(4):
        corr[j * WIDTH:(j + 1) * WIDTH, :] = blocks[j].astype(F32).T
    second = pltpu.make_async_copy(corr, corr_hbm, sem.at[1])
    second.start()
    first.wait()
    second.wait()


def solution(mesh, sizes=(4, 4, 12)):
    ny, nx, nz = sizes
    dma = pltpu.SemaphoreType.DMA

    def body(wavefunctions, hamiltonians, connectivity, face_nodes):
        filtered, blocks = pl.pallas_call(
            lambda *refs: kernel(sizes, *refs),
            out_shape=(
                jax.ShapeDtypeStruct((NODES, WIDTH), F32),
                jax.ShapeDtypeStruct((2, 16, 16, WIDTH), BF16),
            ),
            in_specs=[pl.BlockSpec(memory_space=pltpu.HBM)] * 3,
            out_specs=(pl.BlockSpec(memory_space=pltpu.VMEM),) * 2,
            scratch_shapes=[
                pltpu.VMEM((NODES, WIDTH), BF16),
                pltpu.VMEM((NODES, NODES), BF16),
                pltpu.VMEM((1, NODES), jnp.int32),
                pltpu.VMEM((ROWS, WIDTH), BF16),
                pltpu.VMEM((ROWS, WIDTH), F32),
                pltpu.VMEM((ROWS, WIDTH), BF16),
                pltpu.VMEM((ROWS, WIDTH), BF16),
                pltpu.VMEM((2, ROWS, WIDTH), BF16),
                pltpu.VMEM((ROWS, WIDTH), BF16),
                pltpu.VMEM((ROWS, WIDTH), BF16),
                pltpu.VMEM((2, 2, 96, WIDTH), BF16),
                pltpu.VMEM((2, 2, 96, WIDTH), BF16),
                pltpu.VMEM((96, WIDTH), BF16),
                pltpu.VMEM((2, 16, 16, WIDTH), F32),
                pltpu.VMEM((2, 16, 16, WIDTH), BF16),
                pltpu.VMEM((2, nx * ny - 1, 16, WIDTH), BF16),
                pltpu.VMEM((2, nz, 16, WIDTH), BF16),
                dma((5,)),
                dma((2, 2)), dma((2, 2)),
                dma((3,)),
                pltpu.SemaphoreType.REGULAR((3,)),
                dma((3, 2)), dma((3, 2)), dma((4,)), dma((4,)),
                dma((2,)), dma((2,)), dma((2,)), dma((2,)), dma((2,)), dma((2,)),
            ],
            compiler_params=pltpu.CompilerParams(
                collective_id=0, has_side_effects=True, vmem_limit_bytes=40 << 20
            ),
        )(*[pltpu.with_memory_space_constraint(a, pltpu.HBM) for a in (wavefunctions, hamiltonians, connectivity)])
        return pl.pallas_call(
            finish,
            out_shape=(
                jax.ShapeDtypeStruct((NODES, WIDTH), F32),
                jax.ShapeDtypeStruct((4 * WIDTH, WIDTH), F32),
            ),
            in_specs=[pl.BlockSpec(memory_space=pltpu.VMEM)] * 2,
            out_specs=(pl.BlockSpec(memory_space=pltpu.HBM),) * 2,
            scratch_shapes=[pltpu.VMEM((4 * WIDTH, WIDTH), F32), dma((2,))],
            compiler_params=pltpu.CompilerParams(vmem_limit_bytes=16 << 20),
        )(filtered, blocks.reshape(4, WIDTH, WIDTH))

    return jax.shard_map(
        body,
        mesh=mesh,
        in_specs=(P("cells", "bands"), P("cells", None, None), P("cells", None), P("cells", None)),
        out_specs=(P("cells", "bands"), P(None, "bands")),
        check_vma=False,
    )
```
